128 devices in a mesh: ctx: 8 (over x, z_lo), exp: 16 (over y, z_hi, core).
Axes of the slice: x: 4, y: 4, z: 4 (z_hi: 2, z_lo: 2; z = z_hi * 2 + z_lo), core: 2. Of those that a mesh axis runs over, the one named last changes fastest.
Arguments:
- residual: bfloat16 [16384, 2048], P(('ctx', 'exp')), may hold values from -6 to 6
- queries: bfloat16 [16384, 4096], P('ctx', 'exp'), may hold values from -6.5 to 6.5
- key_rows: bfloat16 [16384, 512], P('ctx'), may hold values from -6.5 to 6.5
- value_rows: bfloat16 [16384, 512], P('ctx'), may hold values from -6 to 6
- segment_ids: int32 [16384], P('ctx'), may hold values from 0 to 31, never falling along the last dimension, each value on 1 to 8704 neighbouring positions
- out_weight: bfloat16 [4096, 2048], P('exp'), may hold values from -0.09375 to 0.09375
- norm_gain: float32 [2048], replicated, may hold values from 0.5 to 1.5
- expert_ids: int32 [16384, 8], P(('ctx', 'exp')), may hold values from 0 to 127, all different within a row; in each aligned block of 128 rows (0 to 127, 128 to 255, ...) at most 16 rows name the same one
- route_weight: float32 [16384, 8], P(('ctx', 'exp')), may hold values from 0.02 to 0.3
- gate_weight: bfloat16 [128, 2048, 768], P(('ctx', 'exp')), may hold values from -0.125 to 0.125
- up_weight: bfloat16 [128, 2048, 768], P(('ctx', 'exp')), may hold values from -0.125 to 0.125
- down_weight: bfloat16 [128, 768, 2048], P(('ctx', 'exp')), may hold values from -0.21875 to 0.21875
Outputs:
- layer_out: bfloat16 [16384, 2048], P(('ctx', 'exp'))
The draws below stay inside these ranges and needn't reach their ends.
Inputs may be any that keep to these rules, and one draw needn't show every extreme that they name: `expert_ids`: within the rows of one device (128 aligned positions), no expert is named by more than 16 rows; some expert is named by exactly 16. `segment_ids`: never falling along positions; each segment covers at most 8704 positions, and some segment exactly 8704.
All inputs are finite; a program needn't handle non-finite values.
Results may differ from the reference program's by a relative error of at most 0.013.
Values may be sent and summed in bfloat16 or wider, within the bound.
No kernel may reach another device: no remote copies, remote signals or barrier semaphores. Data moves between devices by JAX's collectives and lax.ppermute only.
A program may use at most 128 MiB of HBM per device.

```python
import math
import jax
import jax.numpy as jnp
import numpy as np
from jax import lax

D = 2048
HEADS = 32
KV_HEADS = 4
HEAD_DIM = 128
FF_EXP = 768
TOP = 8
ROWS_DEV = 128
HEADS_DEV = 2
LENGTH = 16384
SEG_MOST = 8704
EXPERTS = 128
CAP = 16
SEGS = 32
N_CTX = 8
N_EXP = 16


def draw_queries(key, part):
    fresh_key = jax.random.fold_in(key, 1)
    return jnp.clip(jax.random.normal(fresh_key, (LENGTH, HEADS * HEAD_DIM), jnp.float32), -6.5, 6.5).astype(jnp.bfloat16)


def draw_key_rows(key, part):
    fresh_key = jax.random.fold_in(key, 2)
    return jnp.clip(jax.random.normal(fresh_key, (LENGTH, KV_HEADS * HEAD_DIM), jnp.float32), -6.5, 6.5).astype(jnp.bfloat16)


def shard_levels(key, extent, pieces, smallest, top_value):
    def one(axis_at, parts):
        draws = jax.random.uniform(jax.random.fold_in(jax.random.fold_in(key, 6), axis_at), (parts,), jnp.float32, smallest / len(pieces), top_value / len(pieces))
        return jnp.repeat(jnp.exp(draws), extent[axis_at] // parts).reshape((-1,) + (1,) * (len(extent) - axis_at - 1))

    loudness = one(*pieces[0])
    for cut in pieces[1:]:
        loudness = loudness * one(*cut)
    return loudness


def split_up(number_of, total, reach, skew):
    weights = [(1 << 20) // math.isqrt(standing ** skew) + 1 for standing in range(2, number_of + 1)]
    rest, given = total - reach - (number_of - 1), [1] * (number_of - 1)
    while rest > 0:
        candidates = [i for i in range(number_of - 1) if given[i] < reach]
        whole, budget = sum([weights[i] for i in candidates]), rest
        for i in candidates:
            addition = min(reach - given[i], max(1, budget * weights[i] // whole), rest)
            given[i] = given[i] + addition
            rest = rest - addition
    return np.array([reach] + given)


def ragged(stream_key, count, total, most, skew):
    if count == 2:
        one = jax.random.randint(stream_key, (), max(1, total - most), min(most, total - 1) + 1)
        return jnp.stack([one, total - one])
    sizes = jnp.asarray(split_up(count, total, most, skew), jnp.int32)
    twos = (count - 1) // 2
    donor, sink = sizes[1:1 + 2 * twos:2], sizes[2:2 + 2 * twos:2]
    slack = jnp.minimum(donor - 1, most - sink)
    shifted = jax.random.randint(jax.random.fold_in(stream_key, 1), (twos,), 0, 1 << 20) % (slack + 1)
    sizes = sizes.at[1:1 + 2 * twos:2].set(donor - shifted).at[2:2 + 2 * twos:2].set(sink + shifted)
    return sizes[jax.random.permutation(jax.random.fold_in(stream_key, 2), count)]


def assign_block(own_key, own, number, rows, count, top, limit, skew):
    sequence = jax.random.permutation(own_key, count)
    heavy_load, usual = shares(count, rows * top, limit, skew, True), shares(count, rows * top, limit, skew, False)
    places = jnp.arange(count)

    def named(sizes, offset_by):
        used = int((sizes > 0).sum())
        fixed = max(1, used // 4)
        moved = fixed + (places - fixed + offset_by * (used - fixed)) % max(1, count - fixed)
        return jnp.zeros((count,), jnp.int32).at[sequence[jnp.where(places < fixed, places, moved)]].set(jnp.asarray(sizes, jnp.int32))

    sizes = jnp.where(number % 4 == 0, named(heavy_load, number // 4), named(usual, number - number // 4 - 1))
    mixed = jax.random.permutation(jax.random.fold_in(own, 3), count)
    giver, taker = mixed[0:count // 2 * 2:2], mixed[1:count // 2 * 2:2]
    slack = jnp.minimum(sizes[giver] - 1, limit - sizes[taker]) // 2
    slack = jnp.where((giver == sequence[0]) | (taker == sequence[0]) | (sizes[taker] == 0), 0, jnp.maximum(slack, 0))
    moved = jax.random.randint(jax.random.fold_in(own, 4), (count // 2,), 0, 1 << 20) % (slack + 1)
    sizes = sizes.at[giver].add(-moved).at[taker].add(moved)
    labels = jnp.searchsorted(jnp.cumsum(sizes), jnp.arange(rows * top), side="right").astype(jnp.int32)
    listing = labels.reshape(top, rows).T
    listing = listing[jax.random.permutation(jax.random.fold_in(own, 1), rows)]
    offset_by = jax.random.randint(jax.random.fold_in(own, 2), (rows, 1), 0, top)
    return jnp.take_along_axis(listing, (jnp.arange(top)[None, :] + offset_by) % top, axis=1)


def shares(count, total, limit, skew, full):
    weights = [(1 << 20) // math.isqrt(grade ** skew) + 1 for grade in range(1, count + 1)]
    largest = limit if full else min(limit, max(-(-total // count), total * weights[0] // sum(weights)))
    least = 1 if total - largest >= count - 1 else 0
    given, surplus = [largest] + [least] * (count - 1), total - largest - least * (count - 1)
    while surplus > 0:
        free = [i for i in range(1, count) if given[i] < largest] or [i for i in range(1, count) if given[i] < limit]
        mass, budget = sum([weights[i] for i in free]), surplus
        for i in free:
            more = min(limit - given[i], max(1, budget * weights[i] // mass), surplus)
            given[i] = given[i] + more
            surplus = surplus - more
    return np.array(given)


def normal_values(own_key, extent, deviation, limit, cuts=(), held_as=jnp.bfloat16):
    factor_of = shard_levels(own_key, extent, cuts, -0.22, 0.18) if cuts else 1.0
    values = jax.random.normal(own_key, extent, jnp.float32) * deviation * factor_of
    return jnp.minimum(jnp.maximum(values, -limit), limit).astype(held_as)


def setup_inputs(seed: int = 0) -> dict:
    streams_of = jax.random.split(jax.random.key(seed), 13)
    residual = normal_values(streams_of[0], (LENGTH, D), 1.0, 6.0, ((0, 128),))
    queries = draw_queries(jax.random.fold_in(streams_of[12], 71), 0)
    key_rows = draw_key_rows(jax.random.fold_in(streams_of[12], 71), 0)
    value_rows = normal_values(streams_of[3], (LENGTH, KV_HEADS * HEAD_DIM), 1.0, 6.0, ((0, 8),))
    segment_ids = jnp.searchsorted(jnp.cumsum(ragged(streams_of[4], SEGS, LENGTH, SEG_MOST, 2)), jnp.arange(LENGTH), side="right").astype(jnp.int32)
    out_weight = normal_values(streams_of[5], (HEADS * HEAD_DIM, D), (HEADS * HEAD_DIM) ** -0.5, 0.09375, ((0, 16),))
    norm_gain = jnp.clip(1.0 + 0.1 * jax.random.normal(streams_of[6], (D,), jnp.float32), 0.5, 1.5)
    expert_ids_keys = jax.random.split(jax.random.fold_in(streams_of[7], 1), LENGTH // ROWS_DEV)
    expert_ids_turns = jax.random.permutation(jax.random.fold_in(streams_of[7], 3), LENGTH // ROWS_DEV)
    expert_ids = jax.vmap(lambda own, number: assign_block(jax.random.fold_in(streams_of[7], 2), own, number, ROWS_DEV, EXPERTS, TOP, CAP, 1))(expert_ids_keys, expert_ids_turns).reshape((LENGTH, TOP))
    route_weight = jnp.clip(0.02 + 0.28 * jax.random.uniform(streams_of[8], (LENGTH, TOP), jnp.float32) ** shard_levels(streams_of[8], (LENGTH, TOP), ((0, 128),), -0.2, 0.2), 0.02, 0.3)
    gate_weight = normal_values(streams_of[9], (EXPERTS, D, FF_EXP), D ** -0.5, 0.125, ((0, 128),))
    up_weight = normal_values(streams_of[10], (EXPERTS, D, FF_EXP), D ** -0.5, 0.125, ((0, 128),))
    down_weight = normal_values(streams_of[11], (EXPERTS, FF_EXP, D), FF_EXP ** -0.5, 0.21875, ((0, 128),))
    return dict(residual=residual, queries=queries, key_rows=key_rows, value_rows=value_rows, segment_ids=segment_ids, out_weight=out_weight, norm_gain=norm_gain, expert_ids=expert_ids, route_weight=route_weight, gate_weight=gate_weight, up_weight=up_weight, down_weight=down_weight)


def reference(residual, queries, key_rows, value_rows, segment_ids, out_weight, norm_gain, expert_ids, route_weight, gate_weight, up_weight, down_weight):
    group_size = HEADS // KV_HEADS
    block_rows = min(512, LENGTH)
    window = SEG_MOST + block_rows
    score_scale = 1.0 / math.sqrt(HEAD_DIM)
    key_padded = jnp.concatenate([jnp.zeros((SEG_MOST, KV_HEADS * HEAD_DIM), jnp.bfloat16), key_rows], 0)
    value_padded = jnp.concatenate([jnp.zeros((SEG_MOST, KV_HEADS * HEAD_DIM), jnp.bfloat16), value_rows], 0)
    seg_padded = jnp.concatenate([jnp.full((SEG_MOST,), -1, jnp.int32), segment_ids.astype(jnp.int32)], 0)

    def attend_block(block_index):
        query_start = (block_index * block_rows).astype(jnp.int32)
        query_block = lax.dynamic_slice_in_dim(queries, query_start, block_rows, 0).astype(jnp.float32)
        query_block = query_block.reshape(block_rows, KV_HEADS, group_size, HEAD_DIM)
        key_block = lax.dynamic_slice_in_dim(key_padded, query_start, window, 0).astype(jnp.float32).reshape(window, KV_HEADS, HEAD_DIM)
        value_block = lax.dynamic_slice_in_dim(value_padded, query_start, window, 0).astype(jnp.float32).reshape(window, KV_HEADS, HEAD_DIM)
        key_segs = lax.dynamic_slice_in_dim(seg_padded, query_start, window, 0)
        query_segs = lax.dynamic_slice_in_dim(segment_ids.astype(jnp.int32), query_start, block_rows, 0)
        query_pos = query_start + jnp.arange(block_rows, dtype=jnp.int32)
        key_pos = query_start - SEG_MOST + jnp.arange(window, dtype=jnp.int32)
        visible = (query_segs[:, None] == key_segs[None, :]) & (key_pos[None, :] <= query_pos[:, None])
        scores = jnp.einsum('qkgd,wkd->kgqw', query_block, key_block) * score_scale
        scores = jnp.where(visible[None, None], scores, -jnp.inf)
        row_max = lax.optimization_barrier(jnp.max(scores, axis=-1, keepdims=True))
        unnormed = jnp.exp(scores - row_max)
        totals = lax.optimization_barrier(jnp.sum(unnormed, axis=-1))
        weights = lax.optimization_barrier(unnormed.astype(jnp.bfloat16)).astype(jnp.float32)
        summed = jnp.einsum('kgqw,wkd->qkgd', weights, value_block)
        attended = summed / jnp.transpose(totals, (2, 0, 1))[..., None]
        return attended.reshape(block_rows, HEADS * HEAD_DIM).astype(jnp.bfloat16)
    attended = lax.map(attend_block, jnp.arange(LENGTH // block_rows, dtype=jnp.int32))
    attended = attended.reshape(LENGTH, HEADS * HEAD_DIM)
    group_cols = HEADS_DEV * HEAD_DIM
    mixed_rows = residual.astype(jnp.float32)
    for group_index in range(N_EXP):
        part_cols = attended[:, group_index * group_cols:(group_index + 1) * group_cols]
        part_rows = out_weight[group_index * group_cols:(group_index + 1) * group_cols]
        head_term = jnp.dot(part_cols, part_rows, preferred_element_type=jnp.float32).astype(jnp.bfloat16)
        mixed_rows = mixed_rows + lax.optimization_barrier(head_term).astype(jnp.float32)
    mean_square = lax.optimization_barrier(jnp.mean(mixed_rows * mixed_rows, axis=-1, keepdims=True))
    normed = (mixed_rows * lax.rsqrt(mean_square + 1e-06) * norm_gain).astype(jnp.bfloat16)
    flat_ids = expert_ids.reshape(-1).astype(jnp.int32)
    flat_weight = route_weight.reshape(-1)
    most_rows = N_CTX * N_EXP * CAP

    def per_expert(routed, expert_index):
        hits = flat_ids == expert_index
        chosen = jnp.nonzero(hits, size=most_rows, fill_value=0)[0].astype(jnp.int32)
        valid_rows = (jnp.arange(most_rows) < jnp.sum(hits)).astype(routed.dtype)
        token_index = (chosen // TOP).astype(jnp.int32)
        rows_in = normed[token_index]
        gate_proj = jnp.dot(rows_in, gate_weight[expert_index], preferred_element_type=jnp.float32)
        up_proj = jnp.dot(rows_in, up_weight[expert_index], preferred_element_type=jnp.float32)
        hidden = (jax.nn.silu(gate_proj) * up_proj).astype(jnp.bfloat16)
        expert_out = jnp.dot(hidden, down_weight[expert_index], preferred_element_type=jnp.float32).astype(jnp.bfloat16)
        contrib = expert_out.astype(routed.dtype) * (flat_weight[chosen] * valid_rows)[:, None]
        return (routed.at[token_index].add(contrib), None)
    routed, _ = lax.scan(per_expert, jnp.zeros((LENGTH, D), jnp.float32), jnp.arange(EXPERTS, dtype=jnp.int32))
    return (mixed_rows + routed).astype(jnp.bfloat16)
```

```python
import math

import jax
import jax.numpy as jnp
from jax import lax
from jax.experimental import pallas as pl
from jax.experimental.pallas import tpu as pltpu
from jax.sharding import Mesh
from jax.sharding import PartitionSpec as P

HEAD_DIM = 128
TOP = 8
SEGS = 32
TILE = 128
KEY_TILE = 512
HIDDEN_SCORE = -1e30
SCORE_SCALE = math.log2(math.e) / math.sqrt(HEAD_DIM)

CTX = ("x", "zl")
EXP = ("y", "zh", "c")
ALL = CTX + EXP
PARTS = (4, 2, 4, 2, 2)

CORE_SWAP = [(0, 1), (1, 0)]


def attend_kernel(block, scalars, q_ref, mine_ref, other_ref, o_ref, *scratch):
    kv, max_ref, total_ref, sum_ref, sems = scratch
    step = pl.program_id(0)
    ctx = scalars[SEGS]
    half = block // 2

    @pl.when(step == 0)
    def _():
        core = scalars[SEGS + 1]
        copies = []
        for i, (piece, side) in enumerate(((mine_ref, core), (other_ref, 1 - core))):
            for b in range(8):
                first = pl.multiple_of(b * block + side * half, half)
                copies.append(
                    pltpu.make_async_copy(
                        piece.at[b, pl.ds(2 * TILE, half), :],
                        kv.at[pl.ds(first, half), :],
                        sems.at[8 * i + b],
                    )
                )
        for copy in copies:
            copy.start()
        for copy in copies:
            copy.wait()

    begin = (step // 2) * block + (step % 2) * (block // 2) + ctx * TILE
    low_first = jnp.int32(0)
    low_last = jnp.int32(0)
    for s in range(SEGS):
        start = scalars[s]
        low_first = jnp.where(start <= begin, start, low_first)
        low_last = jnp.where(start <= begin + TILE - 1, start, low_last)
    chunk_begin = low_first // KEY_TILE
    chunk_end = (begin + TILE - 1) // KEY_TILE + 1
    clear_begin = jnp.minimum((low_last + KEY_TILE - 1) // KEY_TILE, chunk_end)
    clear_end = jnp.maximum(clear_begin, (begin + 1) // KEY_TILE)

    query = jnp.concatenate([q_ref[:, :HEAD_DIM], q_ref[:, HEAD_DIM:]], axis=0)
    position = begin + lax.broadcasted_iota(jnp.int32, (TILE, HEAD_DIM), 0)
    lowest = jnp.zeros((TILE, HEAD_DIM), jnp.int32)
    for s in range(SEGS):
        start = scalars[s]
        lowest = jnp.where(position >= start, start, lowest)
    wide = KEY_TILE // HEAD_DIM
    position = jnp.concatenate([position] * wide, axis=1)
    lowest = jnp.concatenate([lowest] * wide, axis=1)

    max_ref[...] = jnp.full_like(max_ref, HIDDEN_SCORE)
    total_ref[...] = jnp.zeros_like(total_ref)
    sum_ref[...] = jnp.zeros_like(sum_ref)

    def attend(chunk, masked):
        first = pl.multiple_of(chunk * KEY_TILE, KEY_TILE)
        key = kv[pl.ds(first, KEY_TILE), :HEAD_DIM]
        value = kv[pl.ds(first, KEY_TILE), HEAD_DIM:]
        scores = (
            lax.dot_general(
                query, key, (((1,), (1,)), ((), ())), preferred_element_type=jnp.float32
            )
            * SCORE_SCALE
        )
        if masked:
            at = first + lax.broadcasted_iota(jnp.int32, (TILE, KEY_TILE), 1)
            visible = (at >= lowest) & (at <= position)
            visible = jnp.concatenate([visible, visible], axis=0)
            scores = jnp.where(visible, scores, HIDDEN_SCORE)
        old_max = max_ref[...]
        new_max = jnp.maximum(old_max, jnp.max(scores, axis=1, keepdims=True))
        rescale = jnp.exp2(old_max - new_max)
        unnormed = jnp.exp2(scores - new_max)
        total_ref[...] = rescale * total_ref[...] + jnp.sum(unnormed, axis=1, keepdims=True)
        max_ref[...] = new_max
        sum_ref[...] = rescale * sum_ref[...] + jnp.dot(
            unnormed.astype(jnp.bfloat16), value, preferred_element_type=jnp.float32
        )

    @pl.loop(clear_begin, clear_end)
    def _(chunk):
        attend(chunk, False)

    before = clear_begin - chunk_begin

    @pl.loop(0, before + chunk_end - clear_end)
    def _(i):
        attend(jnp.where(i < before, chunk_begin + i, clear_end + i - before), True)

    attended = (sum_ref[...] / total_ref[...]).astype(o_ref.dtype)
    o_ref[:, :HEAD_DIM] = attended[:TILE]
    o_ref[:, HEAD_DIM:] = attended[TILE:]


def attend(queries, key_rows, value_rows, starts, x, zl, y, c):
    block, columns = queries.shape
    half = block // 2
    own = jnp.concatenate(
        [
            lax.dynamic_slice(rows, (c * half, y * HEAD_DIM), (half, HEAD_DIM))
            for rows in (key_rows, value_rows)
        ],
        axis=1,
    )
    striped = jnp.transpose(queries.reshape(2, 8, TILE, columns), (1, 0, 2, 3))
    sent = jnp.concatenate(
        [
            striped.reshape(8, 2 * TILE, columns),
            jnp.broadcast_to(own, (8, half, columns)),
        ],
        axis=1,
    )
    mine = lax.all_to_all(sent, CTX, split_axis=0, concat_axis=0, tiled=True)
    other = lax.ppermute(mine, "c", CORE_SWAP)
    scalars = jnp.concatenate([starts, jnp.stack([x * 2 + zl, c]).astype(jnp.int32)])
    any_spec = pl.BlockSpec(memory_space=pl.ANY)
    return pl.pallas_call(
        lambda *refs: attend_kernel(block, *refs),
        out_shape=jax.ShapeDtypeStruct((8, 2 * TILE, columns), jnp.bfloat16),
        grid_spec=pltpu.PrefetchScalarGridSpec(
            num_scalar_prefetch=1,
            grid=(16,),
            in_specs=[
                pl.BlockSpec((None, TILE, columns), lambda i, s: (i // 2, i % 2, 0)),
                any_spec,
                any_spec,
            ],
            out_specs=pl.BlockSpec((None, TILE, columns), lambda i, s: (i // 2, i % 2, 0)),
            scratch_shapes=[
                pltpu.VMEM((8 * block, 2 * HEAD_DIM), jnp.bfloat16),
                pltpu.VMEM((2 * TILE, 1), jnp.float32),
                pltpu.VMEM((2 * TILE, 1), jnp.float32),
                pltpu.VMEM((2 * TILE, HEAD_DIM), jnp.float32),
                pltpu.SemaphoreType.DMA((16,)),
            ],
        ),
        compiler_params=pltpu.CompilerParams(vmem_limit_bytes=32 << 20),
        name="attend",
    )(scalars, mine, mine, other)


def expert_rows(arrived, gate_weight, up_weight, down_weight):
    in_shape = arrived.shape
    flat_rows = arrived.reshape(-1, in_shape[-1])
    gate_proj = jnp.dot(flat_rows, gate_weight[0], preferred_element_type=jnp.float32)
    up_proj = jnp.dot(flat_rows, up_weight[0], preferred_element_type=jnp.float32)
    hidden = (jax.nn.silu(gate_proj) * up_proj).astype(jnp.bfloat16)
    produced = jnp.dot(hidden, down_weight[0], preferred_element_type=jnp.float32).astype(
        jnp.bfloat16
    )
    return produced.reshape(in_shape)


def shards(
    residual,
    queries,
    key_rows,
    value_rows,
    segment_ids,
    out_weight,
    norm_gain,
    expert_ids,
    route_weight,
    gate_weight,
    up_weight,
    down_weight,
):
    ctx_rows, local_cols = queries.shape
    x, zl, y, c = (lax.axis_index(name) for name in ("x", "zl", "y", "c"))
    counts = jnp.sum(
        segment_ids[None, :] < jnp.arange(SEGS, dtype=jnp.int32)[:, None], axis=1, dtype=jnp.int32
    )
    starts = lax.psum(counts, CTX)
    attended = attend(queries, key_rows, value_rows, starts, x, zl, y, c)
    attended = lax.all_to_all(
        attended.reshape(8, 2, TILE, local_cols), CTX, split_axis=0, concat_axis=1
    ).reshape(ctx_rows, local_cols)
    own_rows = residual.shape[0]
    attention_sum = lax.psum_scatter(
        jnp.dot(attended, out_weight, preferred_element_type=jnp.float32).astype(jnp.bfloat16),
        EXP,
        scatter_dimension=0,
        tiled=True,
    ).astype(jnp.float32)
    mixed_rows = residual.astype(jnp.float32) + attention_sum
    mean_square = jnp.mean(mixed_rows * mixed_rows, axis=-1, keepdims=True)
    normed = (mixed_rows * lax.rsqrt(mean_square + 1e-06) * norm_gain).astype(jnp.bfloat16)
    model_width = normed.shape[1]
    expert_count = 128
    capacity = 2 * own_rows * TOP // expert_count
    flat_ids = expert_ids.reshape(-1)
    onehot = (flat_ids[:, None] == jnp.arange(expert_count, dtype=jnp.int32)[None, :]).astype(
        jnp.int32
    )
    slot_index = jnp.sum(jnp.cumsum(onehot, axis=0) * onehot, axis=1) - 1
    repeated = jnp.repeat(normed, TOP, axis=0)
    outgoing = (
        jnp.zeros((expert_count, capacity, model_width), jnp.bfloat16)
        .at[flat_ids, slot_index]
        .set(repeated)
    )
    returned = lax.all_to_all(
        expert_rows(
            lax.all_to_all(outgoing, ALL, split_axis=0, concat_axis=0, tiled=True),
            gate_weight,
            up_weight,
            down_weight,
        ),
        ALL,
        split_axis=0,
        concat_axis=0,
        tiled=True,
    )
    fetched = returned[flat_ids, slot_index].astype(jnp.float32) * route_weight.reshape(-1)[:, None]
    routed = jnp.sum(fetched.reshape(own_rows, TOP, model_width), axis=1)
    return (mixed_rows + routed).astype(jnp.bfloat16)


def solution(mesh):
    fine = Mesh(mesh.devices.reshape(PARTS), ALL)
    return jax.shard_map(
        shards,
        mesh=fine,
        in_specs=(
            P(ALL, None),
            P(CTX, EXP),
            P(CTX, None),
            P(CTX, None),
            P(CTX),
            P(EXP, None),
            P(),
            P(ALL, None),
            P(ALL, None),
            P(ALL, None, None),
            P(ALL, None, None),
            P(ALL, None, None),
        ),
        out_specs=P(ALL, None),
        check_vma=False,
    )
```

```python
import math

import jax
import jax.numpy as jnp
from jax import lax
from jax.experimental import pallas as pl
from jax.experimental.pallas import tpu as pltpu
from jax.sharding import Mesh
from jax.sharding import PartitionSpec as P

HEAD_DIM = 128
TOP = 8
SEGS = 32
TILE = 128
KEY_TILE = 512
HIDDEN_SCORE = -1e30
SCORE_SCALE = math.log2(math.e) / math.sqrt(HEAD_DIM)

CTX = ("x", "zl")
EXP = ("y", "zh", "c")
ALL = CTX + EXP
PARTS = (4, 2, 4, 2, 2)

CORE_SWAP = [(0, 1), (1, 0)]
Z_FLIP = [(0, 3), (3, 0), (1, 2), (2, 1)]
CAPACITY = 16
SLOT_TILE = 256


def attend_kernel(block, scalars, q_ref, mine_ref, other_ref, o_ref, *scratch):
    kv, max_ref, total_ref, sum_ref, sems = scratch
    step = pl.program_id(0)
    ctx = scalars[SEGS]
    half = block // 2

    @pl.when(step == 0)
    def _():
        core = scalars[SEGS + 1]
        copies = []
        for i, (piece, side) in enumerate(((mine_ref, core), (other_ref, 1 - core))):
            for b in range(8):
                first = pl.multiple_of(b * block + side * half, half)
                copies.append(
                    pltpu.make_async_copy(
                        piece.at[b, pl.ds(2 * TILE, half), :],
                        kv.at[pl.ds(first, half), :],
                        sems.at[8 * i + b],
                    )
                )
        for copy in copies:
            copy.start()
        for copy in copies:
            copy.wait()

    begin = (step // 2) * block + (step % 2) * (block // 2) + ctx * TILE
    low_first = jnp.int32(0)
    low_last = jnp.int32(0)
    for s in range(SEGS):
        start = scalars[s]
        low_first = jnp.where(start <= begin, start, low_first)
        low_last = jnp.where(start <= begin + TILE - 1, start, low_last)
    chunk_begin = low_first // KEY_TILE
    chunk_end = (begin + TILE - 1) // KEY_TILE + 1
    clear_begin = jnp.minimum((low_last + KEY_TILE - 1) // KEY_TILE, chunk_end)
    clear_end = jnp.maximum(clear_begin, (begin + 1) // KEY_TILE)

    query = jnp.concatenate([q_ref[:, :HEAD_DIM], q_ref[:, HEAD_DIM:]], axis=0)
    position = begin + lax.broadcasted_iota(jnp.int32, (TILE, HEAD_DIM), 0)
    lowest = jnp.zeros((TILE, HEAD_DIM), jnp.int32)
    for s in range(SEGS):
        start = scalars[s]
        lowest = jnp.where(position >= start, start, lowest)
    wide = KEY_TILE // HEAD_DIM
    position = jnp.concatenate([position] * wide, axis=1)
    lowest = jnp.concatenate([lowest] * wide, axis=1)

    max_ref[...] = jnp.full_like(max_ref, HIDDEN_SCORE)
    total_ref[...] = jnp.zeros_like(total_ref)
    sum_ref[...] = jnp.zeros_like(sum_ref)

    def attend(chunk, masked):
        first = pl.multiple_of(chunk * KEY_TILE, KEY_TILE)
        key = kv[pl.ds(first, KEY_TILE), :HEAD_DIM]
        value = kv[pl.ds(first, KEY_TILE), HEAD_DIM:]
        scores = (
            lax.dot_general(
                query, key, (((1,), (1,)), ((), ())), preferred_element_type=jnp.float32
            )
            * SCORE_SCALE
        )
        if masked:
            at = first + lax.broadcasted_iota(jnp.int32, (TILE, KEY_TILE), 1)
            visible = (at >= lowest) & (at <= position)
            visible = jnp.concatenate([visible, visible], axis=0)
            scores = jnp.where(visible, scores, HIDDEN_SCORE)
        old_max = max_ref[...]
        new_max = jnp.maximum(old_max, jnp.max(scores, axis=1, keepdims=True))
        rescale = jnp.exp2(old_max - new_max)
        unnormed = jnp.exp2(scores - new_max)
        total_ref[...] = rescale * total_ref[...] + jnp.sum(unnormed, axis=1, keepdims=True)
        max_ref[...] = new_max
        sum_ref[...] = rescale * sum_ref[...] + jnp.dot(
            unnormed.astype(jnp.bfloat16), value, preferred_element_type=jnp.float32
        )

    @pl.loop(clear_begin, clear_end)
    def _(chunk):
        attend(chunk, False)

    before = clear_begin - chunk_begin

    @pl.loop(0, before + chunk_end - clear_end)
    def _(i):
        attend(jnp.where(i < before, chunk_begin + i, clear_end + i - before), True)

    attended = (sum_ref[...] / total_ref[...]).astype(o_ref.dtype)
    o_ref[:, :HEAD_DIM] = attended[:TILE]
    o_ref[:, HEAD_DIM:] = attended[TILE:]


def attend(queries, key_rows, value_rows, starts, x, zl, y, c):
    block, columns = queries.shape
    half = block // 2
    own = jnp.concatenate(
        [
            lax.dynamic_slice(rows, (c * half, y * HEAD_DIM), (half, HEAD_DIM))
            for rows in (key_rows, value_rows)
        ],
        axis=1,
    )
    striped = jnp.transpose(queries.reshape(2, 8, TILE, columns), (1, 0, 2, 3))
    sent = jnp.concatenate(
        [
            striped.reshape(8, 2 * TILE, columns),
            jnp.broadcast_to(own, (8, half, columns)),
        ],
        axis=1,
    )
    mine = lax.all_to_all(sent, CTX, split_axis=0, concat_axis=0, tiled=True)
    other = lax.ppermute(mine, "c", CORE_SWAP)
    scalars = jnp.concatenate([starts, jnp.stack([x * 2 + zl, c]).astype(jnp.int32)])
    any_spec = pl.BlockSpec(memory_space=pl.ANY)
    return pl.pallas_call(
        lambda *refs: attend_kernel(block, *refs),
        out_shape=jax.ShapeDtypeStruct((8, 2 * TILE, columns), jnp.bfloat16),
        grid_spec=pltpu.PrefetchScalarGridSpec(
            num_scalar_prefetch=1,
            grid=(16,),
            in_specs=[
                pl.BlockSpec((None, TILE, columns), lambda i, s: (i // 2, i % 2, 0)),
                any_spec,
                any_spec,
            ],
            out_specs=pl.BlockSpec((None, TILE, columns), lambda i, s: (i // 2, i % 2, 0)),
            scratch_shapes=[
                pltpu.VMEM((8 * block, 2 * HEAD_DIM), jnp.bfloat16),
                pltpu.VMEM((2 * TILE, 1), jnp.float32),
                pltpu.VMEM((2 * TILE, 1), jnp.float32),
                pltpu.VMEM((2 * TILE, HEAD_DIM), jnp.float32),
                pltpu.SemaphoreType.DMA((16,)),
            ],
        ),
        compiler_params=pltpu.CompilerParams(vmem_limit_bytes=32 << 20),
        name="attend",
    )(scalars, mine, mine, other)


def mix_kernel(scalars, attended_ref, w0, w1, w2, w3, residual_ref, gain_ref, slots_ref, *refs):
    mixed_ref, outgoing_ref, total, normed = refs
    step = pl.program_id(0)

    @pl.when(step == 0)
    def _():
        total[...] = residual_ref[...].astype(jnp.float32)

    for p, w_ref in enumerate((w0, w1, w2, w3)):

        @pl.when((step >= 4 * p) & (step < 4 * p + 4))
        def _(p=p, w_ref=w_ref):
            block = (step - 4 * p) * 4 + scalars[p]
            total[...] += jnp.dot(
                attended_ref[block], w_ref[...], preferred_element_type=jnp.float32
            )

    @pl.when(step == 15)
    def _():
        mixed = total[...]
        mixed_ref[...] = mixed
        mean_square = jnp.mean(mixed * mixed, axis=-1, keepdims=True)
        normed[...] = (mixed * lax.rsqrt(mean_square + 1e-06) * gain_ref[...]).astype(
            jnp.bfloat16
        )

    @pl.when(step >= 16)
    def _():
        rows = normed.shape[0]
        slot = (step - 16) * SLOT_TILE + lax.broadcasted_iota(jnp.int32, (SLOT_TILE, rows), 0)
        chosen = slots_ref[0:1, :] == slot
        for k in range(1, TOP):
            chosen = chosen | (slots_ref[k : k + 1, :] == slot)
        onehot = jnp.where(chosen, 1.0, 0.0).astype(jnp.bfloat16)
        outgoing_ref[...] = jnp.dot(
            onehot, normed[...], preferred_element_type=jnp.float32
        ).astype(jnp.bfloat16)


def mix(attended, weights, order, residual, norm_gain, slots):
    rows, width = residual.shape
    count = 128 * CAPACITY
    whole = lambda shape: pl.BlockSpec(shape, lambda i, s: (0,) * len(shape))

    def weight_spec(p):
        return pl.BlockSpec((256, width), lambda i, s: (jnp.clip(i - 4 * p, 0, 3), 0))

    return pl.pallas_call(
        mix_kernel,
        out_shape=(
            jax.ShapeDtypeStruct((rows, width), jnp.float32),
            jax.ShapeDtypeStruct((count, width), jnp.bfloat16),
        ),
        grid_spec=pltpu.PrefetchScalarGridSpec(
            num_scalar_prefetch=1,
            grid=(16 + count // SLOT_TILE,),
            in_specs=[whole(attended.shape)]
            + [weight_spec(p) for p in range(4)]
            + [whole((rows, width)), whole((1, width)), whole((TOP, rows))],
            out_specs=(
                whole((rows, width)),
                pl.BlockSpec((SLOT_TILE, width), lambda i, s: (jnp.maximum(i - 16, 0), 0)),
            ),
            scratch_shapes=[
                pltpu.VMEM((rows, width), jnp.float32),
                pltpu.VMEM((rows, width), jnp.bfloat16),
            ],
        ),
        compiler_params=pltpu.CompilerParams(vmem_limit_bytes=32 << 20),
        name="mix",
    )(order, attended, *weights, residual, norm_gain.reshape(1, width), slots)


def combine_kernel(returned_ref, slots_ref, route_ref, mixed_ref, out_ref, total):
    step = pl.program_id(0)

    @pl.when(step == 0)
    def _():
        total[...] = mixed_ref[...]

    rows = total.shape[0]
    slot = step * SLOT_TILE + lax.broadcasted_iota(jnp.int32, (rows, SLOT_TILE), 1)
    share = jnp.zeros((rows, SLOT_TILE), jnp.float32)
    for k in range(TOP):
        share = jnp.where(slots_ref[:, k : k + 1] == slot, route_ref[:, k : k + 1], share)
    high = share.astype(jnp.bfloat16)
    low = (share - high.astype(jnp.float32)).astype(jnp.bfloat16)
    both = jnp.dot(
        jnp.concatenate([high, low], axis=0), returned_ref[...], preferred_element_type=jnp.float32
    )
    total[...] += both[:rows] + both[rows:]

    @pl.when(step == pl.num_programs(0) - 1)
    def _():
        out_ref[...] = total[...].astype(out_ref.dtype)


def combine(returned, slots, route_weight, mixed):
    rows, width = mixed.shape
    whole = lambda shape: pl.BlockSpec(shape, lambda i: (0, 0))
    return pl.pallas_call(
        combine_kernel,
        out_shape=jax.ShapeDtypeStruct((rows, width), jnp.bfloat16),
        grid=(returned.shape[0] // SLOT_TILE,),
        in_specs=[
            pl.BlockSpec((SLOT_TILE, width), lambda i: (i, 0)),
            whole((rows, TOP)),
            whole((rows, TOP)),
            whole((rows, width)),
        ],
        out_specs=whole((rows, width)),
        scratch_shapes=[pltpu.VMEM((rows, width), jnp.float32)],
        compiler_params=pltpu.CompilerParams(vmem_limit_bytes=32 << 20),
        name="combine",
    )(returned, slots, route_weight, mixed)


def expert_rows(arrived, gate_weight, up_weight, down_weight):
    in_shape = arrived.shape
    flat_rows = arrived.reshape(-1, in_shape[-1])
    gate_proj = jnp.dot(flat_rows, gate_weight[0], preferred_element_type=jnp.float32)
    up_proj = jnp.dot(flat_rows, up_weight[0], preferred_element_type=jnp.float32)
    hidden = (jax.nn.silu(gate_proj) * up_proj).astype(jnp.bfloat16)
    produced = jnp.dot(hidden, down_weight[0], preferred_element_type=jnp.float32).astype(
        jnp.bfloat16
    )
    return produced.reshape(in_shape)


def shards(
    residual,
    queries,
    key_rows,
    value_rows,
    segment_ids,
    out_weight,
    norm_gain,
    expert_ids,
    route_weight,
    gate_weight,
    up_weight,
    down_weight,
):
    columns = queries.shape[1]
    x, zl, y, zh, c = (lax.axis_index(name) for name in ALL)
    near = lax.all_gather(out_weight, "y", axis=0, tiled=True)
    far = lax.all_gather(
        lax.ppermute(out_weight, ("zl", "zh"), Z_FLIP), "y", axis=0, tiled=True
    )
    near_other = lax.ppermute(near, "c", CORE_SWAP)
    order = jnp.stack(
        [zh * 2 + c, zh * 2 + 1 - c, (1 - zh) * 2 + c, (1 - zh) * 2 + 1 - c]
    ).astype(jnp.int32)

    flat_ids = expert_ids.reshape(-1)
    onehot = (flat_ids[:, None] == jnp.arange(128, dtype=jnp.int32)[None, :]).astype(jnp.int32)
    slot_index = jnp.sum(jnp.cumsum(onehot, axis=0) * onehot, axis=1) - 1
    slots = (flat_ids * CAPACITY + slot_index).reshape(expert_ids.shape)

    counts = jnp.sum(
        segment_ids[None, :] < jnp.arange(SEGS, dtype=jnp.int32)[:, None], axis=1, dtype=jnp.int32
    )
    starts = lax.psum(counts, CTX)
    attended = attend(queries, key_rows, value_rows, starts, x, zl, y, c)
    attended, far = lax.optimization_barrier((attended, far))
    far_other = lax.ppermute(far, "c", CORE_SWAP)
    attended = lax.all_to_all(
        attended.reshape(8, 2, TILE, columns), CTX, split_axis=0, concat_axis=1
    )
    attended = lax.all_to_all(
        attended.reshape(16, TILE, columns), EXP, split_axis=0, concat_axis=0, tiled=True
    )
    mixed, outgoing = mix(
        attended, (near, near_other, far, far_other), order, residual, norm_gain, slots.T
    )
    returned = lax.all_to_all(
        expert_rows(
            lax.all_to_all(
                outgoing.reshape(128, CAPACITY, -1), ALL, split_axis=0, concat_axis=0, tiled=True
            ),
            gate_weight,
            up_weight,
            down_weight,
        ),
        ALL,
        split_axis=0,
        concat_axis=0,
        tiled=True,
    )
    return combine(returned.reshape(128 * CAPACITY, -1), slots, route_weight, mixed)


def solution(mesh):
    fine = Mesh(mesh.devices.reshape(PARTS), ALL)
    return jax.shard_map(
        shards,
        mesh=fine,
        in_specs=(
            P(ALL, None),
            P(CTX, EXP),
            P(CTX, None),
            P(CTX, None),
            P(CTX),
            P(EXP, None),
            P(),
            P(ALL, None),
            P(ALL, None),
            P(ALL, None, None),
            P(ALL, None, None),
            P(ALL, None, None),
        ),
        out_specs=P(ALL, None),
        check_vma=False,
    )
```

```python
import math

import jax
import jax.numpy as jnp
from jax import lax
from jax.experimental import pallas as pl
from jax.experimental.pallas import tpu as pltpu
from jax.sharding import Mesh
from jax.sharding import PartitionSpec as P

HEAD_DIM = 128
TOP = 8
SEGS = 32
TILE = 128
KEY_TILE = 512
HIDDEN_SCORE = -1e30
SCORE_SCALE = math.log2(math.e) / math.sqrt(HEAD_DIM)

CTX = ("x", "zl")
EXP = ("y", "zh", "c")
ALL = CTX + EXP
PARTS = (4, 2, 4, 2, 2)

CORE_SWAP = [(0, 1), (1, 0)]
Z_FLIP = [(0, 3), (3, 0), (1, 2), (2, 1)]
CAPACITY = 16
SLOT_TILE = 256
WIDTH_TILE = 512
VMEM_LIMIT = 60 << 20


def attend_kernel(block, scalars, q_ref, mine_ref, other_ref, o_ref, *scratch):
    kv, max_ref, total_ref, sum_ref, score_ref, sems = scratch
    step = pl.program_id(0)
    ctx = scalars[SEGS]
    core = scalars[SEGS + 1]
    half = block // 2

    def fetch(b):
        return [
            pltpu.make_async_copy(
                piece.at[b, pl.ds(2 * TILE, half), :],
                kv.at[pl.ds(pl.multiple_of(KEY_TILE + b * block + side * half, half), half), :],
                sems.at[i, b],
            )
            for i, (piece, side) in enumerate(((mine_ref, core), (other_ref, 1 - core)))
        ]

    @pl.when(step == 0)
    def _():
        for b in range(8):
            for copy in fetch(b):
                copy.start()
        kv[:KEY_TILE, :] = jnp.zeros((KEY_TILE, 2 * HEAD_DIM), kv.dtype)

    for b in range(8):

        @pl.when(step == 2 * b)
        def _(b=b):
            for copy in fetch(b):
                copy.wait()

    begin = (step // 2) * block + (step % 2) * half + ctx * TILE
    end = begin + TILE
    lowest_first = jnp.int32(0)
    for s in range(SEGS):
        lowest_first = jnp.where(scalars[s] <= begin, scalars[s], lowest_first)
    chunks = (end - lowest_first + KEY_TILE - 1) // KEY_TILE

    query = jnp.concatenate([q_ref[:, :HEAD_DIM], q_ref[:, HEAD_DIM:]], axis=0)
    position = begin + lax.broadcasted_iota(jnp.int32, (TILE, HEAD_DIM), 0)
    lowest = jnp.zeros((TILE, HEAD_DIM), jnp.int32)
    for s in range(SEGS):
        lowest = jnp.where(position >= scalars[s], scalars[s], lowest)
    wide = KEY_TILE // HEAD_DIM
    lane = lax.broadcasted_iota(jnp.int32, (TILE, KEY_TILE), 1)
    lowest = jnp.concatenate([lowest] * wide, axis=1) - lane
    position = jnp.concatenate([position] * wide, axis=1) - lane

    max_ref[...] = jnp.full_like(max_ref, HIDDEN_SCORE)
    total_ref[...] = jnp.zeros_like(total_ref)
    sum_ref[...] = jnp.zeros_like(sum_ref)

    def rows_of(chunk):
        return pl.ds(pl.multiple_of(end - chunk * KEY_TILE, TILE), KEY_TILE)

    def score(slot, chunk):
        score_ref[slot] = lax.dot_general(
            query,
            kv[rows_of(chunk), :HEAD_DIM],
            (((1,), (1,)), ((), ())),
            preferred_element_type=jnp.float32,
        )

    def accumulate(slot, chunk):
        first = end - (chunk + 1) * KEY_TILE
        visible = (lowest <= first) & (position >= first)
        scores = jnp.where(
            jnp.concatenate([visible, visible], axis=0), score_ref[slot] * SCORE_SCALE, HIDDEN_SCORE
        )
        old_max = max_ref[...]
        new_max = jnp.maximum(old_max, jnp.max(scores, axis=1, keepdims=True))
        rescale = jnp.exp2(old_max - new_max)
        unnormed = jnp.exp2(scores - jnp.concatenate([new_max] * wide, axis=1))
        total_ref[...] = rescale * total_ref[...] + jnp.sum(unnormed, axis=1, keepdims=True)
        max_ref[...] = new_max
        sum_ref[...] = rescale * sum_ref[...] + jnp.dot(
            unnormed.astype(jnp.bfloat16),
            kv[rows_of(chunk), HEAD_DIM:],
            preferred_element_type=jnp.float32,
        )

    score(0, 0)

    @pl.loop(0, chunks // 2)
    def _(i):
        chunk = 2 * i
        score(1, chunk + 1)
        accumulate(0, chunk)
        score(0, jnp.minimum(chunk + 2, chunks - 1))
        accumulate(1, chunk + 1)

    @pl.when(chunks % 2 == 1)
    def _():
        accumulate(0, chunks - 1)

    attended = (sum_ref[...] / total_ref[...]).astype(o_ref.dtype)
    o_ref[:, :HEAD_DIM] = attended[:TILE]
    o_ref[:, HEAD_DIM:] = attended[TILE:]


def gather_keys(queries, key_rows, value_rows, y, c):
    block, columns = queries.shape
    half = block // 2
    own = jnp.concatenate(
        [
            lax.dynamic_slice(rows, (c * half, y * HEAD_DIM), (half, HEAD_DIM))
            for rows in (key_rows, value_rows)
        ],
        axis=1,
    )
    striped = jnp.transpose(queries.reshape(2, 8, TILE, columns), (1, 0, 2, 3))
    sent = jnp.concatenate(
        [
            striped.reshape(8, 2 * TILE, columns),
            jnp.broadcast_to(own, (8, half, columns)),
        ],
        axis=1,
    )
    mine = lax.all_to_all(sent, CTX, split_axis=0, concat_axis=0, tiled=True)
    other = lax.ppermute(mine, "c", CORE_SWAP)
    return mine, other


def attend(scalars, mine, other, block):
    columns = mine.shape[2]
    any_spec = pl.BlockSpec(memory_space=pl.ANY)
    tile_spec = pl.BlockSpec((None, TILE, columns), lambda i, s: (i // 2, i % 2, 0))
    return pl.pallas_call(
        lambda *refs: attend_kernel(block, *refs),
        out_shape=jax.ShapeDtypeStruct((8, 2 * TILE, columns), jnp.bfloat16),
        grid_spec=pltpu.PrefetchScalarGridSpec(
            num_scalar_prefetch=1,
            grid=(16,),
            in_specs=[tile_spec, any_spec, any_spec],
            out_specs=tile_spec,
            scratch_shapes=[
                pltpu.VMEM((KEY_TILE + 8 * block, 2 * HEAD_DIM), jnp.bfloat16),
                pltpu.VMEM((2 * TILE, HEAD_DIM), jnp.float32),
                pltpu.VMEM((2 * TILE, HEAD_DIM), jnp.float32),
                pltpu.VMEM((2 * TILE, HEAD_DIM), jnp.float32),
                pltpu.VMEM((2, 2 * TILE, KEY_TILE), jnp.float32),
                pltpu.SemaphoreType.DMA((2, 8)),
            ],
        ),
        compiler_params=pltpu.CompilerParams(vmem_limit_bytes=VMEM_LIMIT),
        cost_estimate=pl.CostEstimate(
            flops=8 << 30, bytes_accessed=12 << 20, transcendentals=16 << 20
        ),
        name="attend",
    )(scalars, mine, mine, other)


def place_rows(slots_ref, normed, first, out_ref):
    count, rows = out_ref.shape[0], normed.shape[0]
    slot = first + lax.broadcasted_iota(jnp.int32, (count, rows), 0)
    chosen = slots_ref[0:1, :] == slot
    for k in range(1, TOP):
        chosen = chosen | (slots_ref[k : k + 1, :] == slot)
    onehot = jnp.where(chosen, 1.0, 0.0).astype(jnp.bfloat16)
    out_ref[...] = jnp.dot(onehot, normed, preferred_element_type=jnp.float32).astype(
        out_ref.dtype
    )


def mix_kernel(scalars, attended_ref, w0, w1, w2, w3, residual_ref, gain_ref, slots_ref, *refs):
    mixed_ref, normed_ref, outgoing_ref = refs
    step = pl.program_id(0)
    tiles = mixed_ref.shape[1] // WIDTH_TILE

    for n in range(tiles):

        @pl.when(step == n)
        def _(n=n):
            columns = slice(n * WIDTH_TILE, (n + 1) * WIDTH_TILE)
            total = residual_ref[:, columns].astype(jnp.float32)
            for p, w_ref in enumerate((w0, w1, w2, w3)):
                rows = jnp.concatenate(
                    [attended_ref[4 * k + scalars[p]] for k in range(4)], axis=1
                )
                total += jnp.dot(rows, w_ref[...], preferred_element_type=jnp.float32)
            mixed_ref[:, columns] = total

    @pl.when(step == tiles - 1)
    def _():
        mixed = mixed_ref[...]
        mean_square = jnp.mean(mixed * mixed, axis=-1, keepdims=True)
        normed_ref[...] = (mixed * lax.rsqrt(mean_square + 1e-06) * gain_ref[...]).astype(
            jnp.bfloat16
        )

    @pl.when(step >= tiles)
    def _():
        place_rows(slots_ref, normed_ref[...], (step - tiles) * SLOT_TILE, outgoing_ref)


def whole(shape):
    return pl.BlockSpec(shape, lambda i, *s: (0,) * len(shape))


def mix(attended, weights, order, residual, norm_gain, slots):
    rows, width = residual.shape
    tiles = width // WIDTH_TILE
    count = 128 * CAPACITY // 2

    return pl.pallas_call(
        mix_kernel,
        out_shape=(
            jax.ShapeDtypeStruct((rows, width), jnp.float32),
            jax.ShapeDtypeStruct((rows, width), jnp.bfloat16),
            jax.ShapeDtypeStruct((count, width), jnp.bfloat16),
        ),
        grid_spec=pltpu.PrefetchScalarGridSpec(
            num_scalar_prefetch=1,
            grid=(tiles + count // SLOT_TILE,),
            in_specs=[whole(attended.shape)]
            + [
                pl.BlockSpec((1024, WIDTH_TILE), lambda i, s: (0, jnp.minimum(i, tiles - 1)))
                for _ in weights
            ]
            + [whole((rows, width)), whole((1, width)), whole((TOP, rows))],
            out_specs=(
                whole((rows, width)),
                whole((rows, width)),
                pl.BlockSpec((SLOT_TILE, width), lambda i, s: (jnp.maximum(i - tiles, 0), 0)),
            ),
        ),
        compiler_params=pltpu.CompilerParams(vmem_limit_bytes=VMEM_LIMIT),
        cost_estimate=pl.CostEstimate(
            flops=3 << 30, bytes_accessed=24 << 20, transcendentals=0
        ),
        name="mix",
    )(order, attended, *weights, residual, norm_gain.reshape(1, width), slots)


def place(normed, slots, first):
    rows, width = normed.shape
    count = 128 * CAPACITY // 2

    def kernel(normed_ref, slots_ref, out_ref):
        place_rows(
            slots_ref, normed_ref[...], first + pl.program_id(0) * SLOT_TILE, out_ref
        )

    return pl.pallas_call(
        kernel,
        out_shape=jax.ShapeDtypeStruct((count, width), jnp.bfloat16),
        grid=(count // SLOT_TILE,),
        in_specs=[whole((rows, width)), whole((TOP, rows))],
        out_specs=pl.BlockSpec((SLOT_TILE, width), lambda i: (i, 0)),
        compiler_params=pltpu.CompilerParams(vmem_limit_bytes=VMEM_LIMIT),
        cost_estimate=pl.CostEstimate(
            flops=1 << 29, bytes_accessed=5 << 20, transcendentals=0
        ),
        name="place",
    )(normed, slots)


def combine(returned, slots, route_weight, base, first, dtype):
    rows, width = base.shape
    count = returned.shape[0]

    def kernel(returned_ref, slots_ref, route_ref, base_ref, out_ref, shares):
        @pl.when(pl.program_id(0) == 0)
        def _():
            slot = first + lax.broadcasted_iota(jnp.int32, (rows, count), 1)
            share = jnp.zeros((rows, count), jnp.float32)
            for k in range(TOP):
                share = jnp.where(
                    slots_ref[:, k : k + 1] == slot, route_ref[:, k : k + 1], share
                )
            high = share.astype(jnp.bfloat16)
            shares[:rows, :] = high
            shares[rows:, :] = (share - high.astype(jnp.float32)).astype(jnp.bfloat16)

        both = jnp.dot(shares[...], returned_ref[...], preferred_element_type=jnp.float32)
        out_ref[...] = (base_ref[...] + (both[:rows] + both[rows:])).astype(out_ref.dtype)

    tile = lambda height: pl.BlockSpec((height, WIDTH_TILE), lambda i: (0, i))
    return pl.pallas_call(
        kernel,
        out_shape=jax.ShapeDtypeStruct((rows, width), dtype),
        grid=(width // WIDTH_TILE,),
        in_specs=[tile(count), whole((rows, TOP)), whole((rows, TOP)), tile(rows)],
        out_specs=tile(rows),
        scratch_shapes=[pltpu.VMEM((2 * rows, count), jnp.bfloat16)],
        compiler_params=pltpu.CompilerParams(vmem_limit_bytes=VMEM_LIMIT),
        cost_estimate=pl.CostEstimate(
            flops=1 << 30, bytes_accessed=6 << 20, transcendentals=0
        ),
        name="combine",
    )(returned, slots, route_weight, base)


def expert_rows(arrived, gate_weight, up_weight, down_weight):
    in_shape = arrived.shape
    flat_rows = arrived.reshape(-1, in_shape[-1])
    gate_proj = jnp.dot(flat_rows, gate_weight[0], preferred_element_type=jnp.float32)
    up_proj = jnp.dot(flat_rows, up_weight[0], preferred_element_type=jnp.float32)
    hidden = (jax.nn.silu(gate_proj) * up_proj).astype(jnp.bfloat16)
    produced = jnp.dot(hidden, down_weight[0], preferred_element_type=jnp.float32).astype(
        jnp.bfloat16
    )
    return produced.reshape(in_shape)


def shards(
    residual,
    queries,
    key_rows,
    value_rows,
    segment_ids,
    out_weight,
    norm_gain,
    expert_ids,
    route_weight,
    gate_weight,
    up_weight,
    down_weight,
):
    columns = queries.shape[1]
    x, zl, y, zh, c = (lax.axis_index(name) for name in ALL)
    near = lax.all_gather(out_weight, "y", axis=0, tiled=True)
    near_other = lax.ppermute(near, "c", CORE_SWAP)
    order = jnp.stack(
        [zh * 2 + c, zh * 2 + 1 - c, (1 - zh) * 2 + c, (1 - zh) * 2 + 1 - c]
    ).astype(jnp.int32)

    flat_ids = expert_ids.reshape(-1)
    onehot = (flat_ids[:, None] == jnp.arange(128, dtype=jnp.int32)[None, :]).astype(jnp.int32)
    slot_index = jnp.sum(jnp.cumsum(onehot, axis=0) * onehot, axis=1) - 1
    half = CAPACITY // 2
    slots = (
        slot_index // half * (128 * half) + flat_ids * half + slot_index % half
    ).reshape(expert_ids.shape)

    counts = jnp.sum(
        segment_ids[None, :] < jnp.arange(SEGS, dtype=jnp.int32)[:, None], axis=1, dtype=jnp.int32
    )
    starts = lax.psum(counts, CTX)
    mine, other = gather_keys(queries, key_rows, value_rows, y, c)
    late_weight, mine = lax.optimization_barrier((out_weight, mine))
    far = lax.all_gather(
        lax.ppermute(late_weight, ("zl", "zh"), Z_FLIP), "y", axis=0, tiled=True
    )
    scalars = jnp.concatenate([starts, jnp.stack([x * 2 + zl, c]).astype(jnp.int32)])
    attended = attend(scalars, mine, other, queries.shape[0])
    attended, far = lax.optimization_barrier((attended, far))
    far_other = lax.ppermute(far, "c", CORE_SWAP)
    attended = lax.all_to_all(
        attended.reshape(8, 2, TILE, columns), CTX, split_axis=0, concat_axis=1
    )
    attended = lax.all_to_all(
        attended.reshape(16, TILE, columns), EXP, split_axis=0, concat_axis=0, tiled=True
    )
    mixed, normed, outgoing = mix(
        attended, (near, near_other, far, far_other), order, residual, norm_gain, slots.T
    )
    count, width = outgoing.shape

    def exchange(rows):
        return lax.all_to_all(
            rows.reshape(128, half, width), ALL, split_axis=0, concat_axis=0, tiled=True
        )

    def experts(rows):
        return expert_rows(rows, gate_weight, up_weight, down_weight)

    arrived_0 = exchange(outgoing)
    arrived_1 = exchange(place(normed, slots.T, count))
    returned_0 = exchange(experts(arrived_0)).reshape(count, width)
    returned_1 = exchange(experts(arrived_1)).reshape(count, width)
    partial = combine(returned_0, slots, route_weight, mixed, 0, jnp.float32)
    return combine(returned_1, slots, route_weight, partial, count, jnp.bfloat16)


def solution(mesh):
    fine = Mesh(mesh.devices.reshape(PARTS), ALL)
    return jax.shard_map(
        shards,
        mesh=fine,
        in_specs=(
            P(ALL, None),
            P(CTX, EXP),
            P(CTX, None),
            P(CTX, None),
            P(CTX),
            P(EXP, None),
            P(),
            P(ALL, None),
            P(ALL, None),
            P(ALL, None, None),
            P(ALL, None, None),
            P(ALL, None, None),
        ),
        out_specs=P(ALL, None),
        check_vma=False,
    )
```

```python
import math

import jax
import jax.numpy as jnp
from jax import lax
from jax.experimental import pallas as pl
from jax.experimental.pallas import tpu as pltpu
from jax.sharding import Mesh
from jax.sharding import PartitionSpec as P

HEAD_DIM = 128
TOP = 8
SEGS = 32
TILE = 128
KEY_TILE = 512
UNROLL = 4
HIDDEN_SCORE = -1e30
SCORE_SCALE = math.log2(math.e) / math.sqrt(HEAD_DIM)

CTX = ("x", "zl")
EXP = ("yh", "yl", "zh", "c")
ALL = CTX + EXP
PARTS = (4, 2, 2, 2, 2, 2)
OWNER = ("yl", "zh", "c", "yh")

CORE_SWAP = [(0, 1), (1, 0)]
CAPACITY = 16
SLOT_TILE = 256
WIDTH_TILE = 512
VMEM_LIMIT = 60 << 20


def attend_kernel(block, scalars, q_ref, mine_ref, other_ref, o_ref, *scratch):
    kv, max_ref, total_ref, sum_ref, score_ref, sems = scratch
    step = pl.program_id(0)
    ctx = scalars[SEGS]
    core = scalars[SEGS + 1]
    half = block // 2

    def fetch(b):
        return [
            pltpu.make_async_copy(
                piece.at[b, pl.ds(2 * TILE, half), :],
                kv.at[pl.ds(pl.multiple_of(KEY_TILE + b * block + side * half, half), half), :],
                sems.at[i, b],
            )
            for i, (piece, side) in enumerate(((mine_ref, core), (other_ref, 1 - core)))
        ]

    @pl.when(step == 0)
    def _():
        for b in range(8):
            for copy in fetch(b):
                copy.start()
        kv[:KEY_TILE, :] = jnp.zeros((KEY_TILE, 2 * HEAD_DIM), kv.dtype)

    for b in range(8):

        @pl.when(step == 2 * b)
        def _(b=b):
            for copy in fetch(b):
                copy.wait()

    begin = (step // 2) * block + (step % 2) * half + ctx * TILE
    end = begin + TILE
    lowest_first = jnp.int32(0)
    for s in range(SEGS):
        lowest_first = jnp.where(scalars[s] <= begin, scalars[s], lowest_first)
    chunks = (end - lowest_first + KEY_TILE - 1) // KEY_TILE

    query = jnp.concatenate([q_ref[:, :HEAD_DIM], q_ref[:, HEAD_DIM:]], axis=0)
    position = begin + lax.broadcasted_iota(jnp.int32, (TILE, HEAD_DIM), 0)
    lowest = jnp.zeros((TILE, HEAD_DIM), jnp.int32)
    for s in range(SEGS):
        lowest = jnp.where(position >= scalars[s], scalars[s], lowest)
    wide = KEY_TILE // HEAD_DIM
    lane = lax.broadcasted_iota(jnp.int32, (TILE, KEY_TILE), 1)
    lowest = jnp.concatenate([lowest] * wide, axis=1) - lane
    position = jnp.concatenate([position] * wide, axis=1) - lane

    max_ref[...] = jnp.full_like(max_ref, HIDDEN_SCORE)
    total_ref[...] = jnp.zeros_like(total_ref)
    sum_ref[...] = jnp.zeros_like(sum_ref)

    def rows_of(chunk):
        return pl.ds(pl.multiple_of(end - chunk * KEY_TILE, TILE), KEY_TILE)

    def score(slot, chunk):
        score_ref[slot] = lax.dot_general(
            query,
            kv[rows_of(chunk), :HEAD_DIM],
            (((1,), (1,)), ((), ())),
            preferred_element_type=jnp.float32,
        )

    def accumulate(slot, chunk):
        first = end - (chunk + 1) * KEY_TILE
        visible = (lowest <= first) & (position >= first)
        scores = jnp.where(
            jnp.concatenate([visible, visible], axis=0), score_ref[slot] * SCORE_SCALE, HIDDEN_SCORE
        )
        old_max = max_ref[...]
        new_max = jnp.maximum(old_max, jnp.max(scores, axis=1, keepdims=True))
        rescale = jnp.exp2(old_max - new_max)
        unnormed = jnp.exp2(scores - jnp.concatenate([new_max] * wide, axis=1))
        total_ref[...] = rescale * total_ref[...] + jnp.sum(unnormed, axis=1, keepdims=True)
        max_ref[...] = new_max
        sum_ref[...] = rescale * sum_ref[...] + jnp.dot(
            unnormed.astype(jnp.bfloat16),
            kv[rows_of(chunk), HEAD_DIM:],
            preferred_element_type=jnp.float32,
        )

    last = chunks - 1
    score(0, 0)

    def run(first, count):
        for i in range(count):
            score((i + 1) % 2, jnp.minimum(first + i + 1, last))
            accumulate(i % 2, first + i)

    @pl.loop(0, chunks // UNROLL)
    def _(i):
        run(UNROLL * i, UNROLL)

    if UNROLL == 4:

        @pl.when(chunks % 4 >= 2)
        def _():
            run(chunks // 4 * 4, 2)

    @pl.when(chunks % 2 == 1)
    def _():
        accumulate(0, last)

    attended = (sum_ref[...] / total_ref[...]).astype(o_ref.dtype)
    o_ref[:, :HEAD_DIM] = attended[:TILE]
    o_ref[:, HEAD_DIM:] = attended[TILE:]


def gather_keys(queries, key_rows, value_rows, y, c):
    block, columns = queries.shape
    half = block // 2
    own = jnp.concatenate(
        [
            lax.dynamic_slice(rows, (c * half, y * HEAD_DIM), (half, HEAD_DIM))
            for rows in (key_rows, value_rows)
        ],
        axis=1,
    )
    striped = jnp.transpose(queries.reshape(2, 8, TILE, columns), (1, 0, 2, 3))
    sent = jnp.concatenate(
        [
            striped.reshape(8, 2 * TILE, columns),
            jnp.broadcast_to(own, (8, half, columns)),
        ],
        axis=1,
    )
    mine = lax.all_to_all(sent, CTX, split_axis=0, concat_axis=0, tiled=True)
    other = lax.ppermute(mine, "c", CORE_SWAP)
    return mine, other


def attend(scalars, mine, other, block):
    columns = mine.shape[2]
    any_spec = pl.BlockSpec(memory_space=pl.ANY)
    tile_spec = pl.BlockSpec((None, TILE, columns), lambda i, s: (i // 2, i % 2, 0))
    return pl.pallas_call(
        lambda *refs: attend_kernel(block, *refs),
        out_shape=jax.ShapeDtypeStruct((8, 2 * TILE, columns), jnp.bfloat16),
        grid_spec=pltpu.PrefetchScalarGridSpec(
            num_scalar_prefetch=1,
            grid=(16,),
            in_specs=[tile_spec, any_spec, any_spec],
            out_specs=tile_spec,
            scratch_shapes=[
                pltpu.VMEM((KEY_TILE + 8 * block, 2 * HEAD_DIM), jnp.bfloat16),
                pltpu.VMEM((2 * TILE, HEAD_DIM), jnp.float32),
                pltpu.VMEM((2 * TILE, HEAD_DIM), jnp.float32),
                pltpu.VMEM((2 * TILE, HEAD_DIM), jnp.float32),
                pltpu.VMEM((2, 2 * TILE, KEY_TILE), jnp.float32),
                pltpu.SemaphoreType.DMA((2, 8)),
            ],
        ),
        compiler_params=pltpu.CompilerParams(vmem_limit_bytes=VMEM_LIMIT),
        cost_estimate=pl.CostEstimate(
            flops=8 << 30, bytes_accessed=12 << 20, transcendentals=16 << 20
        ),
        name="attend",
    )(scalars, mine, mine, other)


def place_rows(slots_ref, normed, first, out_ref):
    count, rows = out_ref.shape[0], normed.shape[0]
    slot = first + lax.broadcasted_iota(jnp.int32, (count, rows), 0)
    chosen = slots_ref[0:1, :] == slot
    for k in range(1, TOP):
        chosen = chosen | (slots_ref[k : k + 1, :] == slot)
    onehot = jnp.where(chosen, 1.0, 0.0).astype(jnp.bfloat16)
    out_ref[...] = jnp.dot(onehot, normed, preferred_element_type=jnp.float32).astype(
        out_ref.dtype
    )


def mix_kernel(scalars, attended_ref, w0, w1, residual_ref, gain_ref, slots_ref, *refs):
    mixed_ref, normed_ref, outgoing_ref = refs
    step = pl.program_id(0)
    tiles = mixed_ref.shape[1] // WIDTH_TILE

    for n in range(tiles):

        @pl.when(step == n)
        def _(n=n):
            columns = slice(n * WIDTH_TILE, (n + 1) * WIDTH_TILE)
            total = residual_ref[:, columns].astype(jnp.float32)
            for p, w_ref in enumerate((w0, w1)):
                rows = jnp.concatenate(
                    [
                        attended_ref[k % 4 * 4 + scalars[p] * 2 + k // 4]
                        for k in range(8)
                    ],
                    axis=1,
                )
                total += jnp.dot(rows, w_ref[...], preferred_element_type=jnp.float32)
            mixed_ref[:, columns] = total

    @pl.when(step == tiles - 1)
    def _():
        mixed = mixed_ref[...]
        mean_square = jnp.mean(mixed * mixed, axis=-1, keepdims=True)
        normed_ref[...] = (mixed * lax.rsqrt(mean_square + 1e-06) * gain_ref[...]).astype(
            jnp.bfloat16
        )

    @pl.when(step >= tiles)
    def _():
        place_rows(slots_ref, normed_ref[...], (step - tiles) * SLOT_TILE, outgoing_ref)


def whole(shape):
    return pl.BlockSpec(shape, lambda i, *s: (0,) * len(shape))


def mix(attended, weights, order, residual, norm_gain, slots):
    rows, width = residual.shape
    tiles = width // WIDTH_TILE
    count = 128 * CAPACITY // 2

    return pl.pallas_call(
        mix_kernel,
        out_shape=(
            jax.ShapeDtypeStruct((rows, width), jnp.float32),
            jax.ShapeDtypeStruct((rows, width), jnp.bfloat16),
            jax.ShapeDtypeStruct((count, width), jnp.bfloat16),
        ),
        grid_spec=pltpu.PrefetchScalarGridSpec(
            num_scalar_prefetch=1,
            grid=(tiles + count // SLOT_TILE,),
            in_specs=[whole(attended.shape)]
            + [
                pl.BlockSpec((2048, WIDTH_TILE), lambda i, s: (0, jnp.minimum(i, tiles - 1)))
                for _ in weights
            ]
            + [whole((rows, width)), whole((1, width)), whole((TOP, rows))],
            out_specs=(
                whole((rows, width)),
                whole((rows, width)),
                pl.BlockSpec((SLOT_TILE, width), lambda i, s: (jnp.maximum(i - tiles, 0), 0)),
            ),
        ),
        compiler_params=pltpu.CompilerParams(vmem_limit_bytes=VMEM_LIMIT),
        cost_estimate=pl.CostEstimate(
            flops=3 << 30, bytes_accessed=24 << 20, transcendentals=0
        ),
        name="mix",
    )(order, attended, *weights, residual, norm_gain.reshape(1, width), slots)


def place(normed, slots, first):
    rows, width = normed.shape
    count = 128 * CAPACITY // 2

    def kernel(normed_ref, slots_ref, out_ref):
        place_rows(
            slots_ref, normed_ref[...], first + pl.program_id(0) * SLOT_TILE, out_ref
        )

    return pl.pallas_call(
        kernel,
        out_shape=jax.ShapeDtypeStruct((count, width), jnp.bfloat16),
        grid=(count // SLOT_TILE,),
        in_specs=[whole((rows, width)), whole((TOP, rows))],
        out_specs=pl.BlockSpec((SLOT_TILE, width), lambda i: (i, 0)),
        compiler_params=pltpu.CompilerParams(vmem_limit_bytes=VMEM_LIMIT),
        cost_estimate=pl.CostEstimate(
            flops=1 << 29, bytes_accessed=5 << 20, transcendentals=0
        ),
        name="place",
    )(normed, slots)


def share_rows(slots_ref, route_ref, first, count):
    rows = slots_ref.shape[0]
    slot = first + lax.broadcasted_iota(jnp.int32, (rows, count), 1)
    share = jnp.zeros((rows, count), jnp.float32)
    for k in range(TOP):
        share = jnp.where(slots_ref[:, k : k + 1] == slot, route_ref[:, k : k + 1], share)
    high = share.astype(jnp.bfloat16)
    low = (share - high.astype(jnp.float32)).astype(jnp.bfloat16)
    return jnp.concatenate([high, low], axis=0)


def add_routed(shares, returned_ref, base_ref, out_ref):
    rows = base_ref.shape[0]
    both = jnp.dot(shares, returned_ref[...], preferred_element_type=jnp.float32)
    out_ref[...] = (base_ref[...] + (both[:rows] + both[rows:])).astype(out_ref.dtype)


def column_tile(height):
    return pl.BlockSpec((height, WIDTH_TILE), lambda i: (0, i))


COMBINE_PARAMS = dict(
    compiler_params=pltpu.CompilerParams(vmem_limit_bytes=VMEM_LIMIT),
    cost_estimate=pl.CostEstimate(flops=1 << 30, bytes_accessed=6 << 20, transcendentals=0),
)


def combine_first(returned, slots, route_weight, base):
    rows, width = base.shape
    count = returned.shape[0]

    def kernel(returned_ref, slots_ref, route_ref, base_ref, out_ref, late_ref, shares):
        @pl.when(pl.program_id(0) == 0)
        def _():
            shares[...] = share_rows(slots_ref, route_ref, 0, count)
            late_ref[...] = share_rows(slots_ref, route_ref, count, count)

        add_routed(shares[...], returned_ref, base_ref, out_ref)

    return pl.pallas_call(
        kernel,
        out_shape=(
            jax.ShapeDtypeStruct((rows, width), jnp.float32),
            jax.ShapeDtypeStruct((2 * rows, count), jnp.bfloat16),
        ),
        grid=(width // WIDTH_TILE,),
        in_specs=[column_tile(count), whole((rows, TOP)), whole((rows, TOP)), column_tile(rows)],
        out_specs=(column_tile(rows), whole((2 * rows, count))),
        scratch_shapes=[pltpu.VMEM((2 * rows, count), jnp.bfloat16)],
        name="combine_first",
        **COMBINE_PARAMS,
    )(returned, slots, route_weight, base)


def combine_last(returned, shares, base):
    rows, width = base.shape
    count = returned.shape[0]

    def kernel(returned_ref, shares_ref, base_ref, out_ref):
        add_routed(shares_ref[...], returned_ref, base_ref, out_ref)

    return pl.pallas_call(
        kernel,
        out_shape=jax.ShapeDtypeStruct((rows, width), jnp.bfloat16),
        grid=(width // WIDTH_TILE,),
        in_specs=[column_tile(count), whole((2 * rows, count)), column_tile(rows)],
        out_specs=column_tile(rows),
        name="combine_last",
        **COMBINE_PARAMS,
    )(returned, shares, base)


def expert_rows(arrived, gate_weight, up_weight, down_weight):
    in_shape = arrived.shape
    flat_rows = arrived.reshape(-1, in_shape[-1])
    gate_proj = jnp.dot(flat_rows, gate_weight[0], preferred_element_type=jnp.float32)
    up_proj = jnp.dot(flat_rows, up_weight[0], preferred_element_type=jnp.float32)
    hidden = (jax.nn.silu(gate_proj) * up_proj).astype(jnp.bfloat16)
    produced = jnp.dot(hidden, down_weight[0], preferred_element_type=jnp.float32).astype(
        jnp.bfloat16
    )
    return produced.reshape(in_shape)


def shards(
    residual,
    queries,
    key_rows,
    value_rows,
    segment_ids,
    out_weight,
    norm_gain,
    expert_ids,
    route_weight,
    gate_weight,
    up_weight,
    down_weight,
):
    columns = queries.shape[1]
    x, zl, yh, yl, zh, c = (lax.axis_index(name) for name in ALL)
    near = lax.all_gather(out_weight, ("yh", "yl", "zh"), axis=0, tiled=True)
    order = jnp.stack([c, 1 - c]).astype(jnp.int32)

    flat_ids = expert_ids.reshape(-1)
    onehot = (flat_ids[:, None] == jnp.arange(128, dtype=jnp.int32)[None, :]).astype(jnp.int32)
    slot_index = jnp.sum(jnp.cumsum(onehot, axis=0) * onehot, axis=1) - 1
    half = CAPACITY // 2
    slots = (
        slot_index // half * (128 * half) + flat_ids * half + slot_index % half
    ).reshape(expert_ids.shape)

    counts = jnp.sum(
        segment_ids[None, :] < jnp.arange(SEGS, dtype=jnp.int32)[:, None], axis=1, dtype=jnp.int32
    )
    starts = lax.psum(counts, CTX)
    mine, other = gather_keys(queries, key_rows, value_rows, yh * 2 + yl, c)
    scalars = jnp.concatenate([starts, jnp.stack([x * 2 + zl, c]).astype(jnp.int32)])
    attended = attend(scalars, mine, other, queries.shape[0])
    attended = lax.all_to_all(attended, CTX, split_axis=0, concat_axis=0, tiled=True)
    attended, near = lax.optimization_barrier((attended, near))
    near_other = lax.ppermute(near, "c", CORE_SWAP)
    attended = lax.all_to_all(
        attended.reshape(16, TILE, columns), OWNER, split_axis=0, concat_axis=0, tiled=True
    )
    mixed, normed, outgoing = mix(
        attended, (near, near_other), order, residual, norm_gain, slots.T
    )
    count, width = outgoing.shape

    def exchange(rows):
        return lax.all_to_all(
            rows.reshape(128, half, width), ALL, split_axis=0, concat_axis=0, tiled=True
        )

    def experts(rows):
        return expert_rows(rows, gate_weight, up_weight, down_weight)

    arrived_0 = exchange(outgoing)
    arrived_1 = exchange(place(normed, slots.T, count))
    returned_0 = exchange(experts(arrived_0)).reshape(count, width)
    returned_1 = exchange(experts(arrived_1)).reshape(count, width)
    partial, shares = combine_first(returned_0, slots, route_weight, mixed)
    return combine_last(returned_1, shares, partial)


def solution(mesh):
    fine = Mesh(mesh.devices.reshape(PARTS), ALL)
    return jax.shard_map(
        shards,
        mesh=fine,
        in_specs=(
            P(ALL, None),
            P(CTX, EXP),
            P(CTX, None),
            P(CTX, None),
            P(CTX),
            P(EXP, None),
            P(),
            P(ALL, None),
            P(ALL, None),
            P(ALL, None, None),
            P(ALL, None, None),
            P(ALL, None, None),
        ),
        out_specs=P(ALL, None),
        check_vma=False,
    )
```

```python
import math

import jax
import jax.numpy as jnp
from jax import lax
from jax.experimental import pallas as pl
from jax.experimental.pallas import tpu as pltpu
from jax.sharding import Mesh
from jax.sharding import PartitionSpec as P

HEAD_DIM = 128
TOP = 8
SEGS = 32
TILE = 128
KEY_TILE = 512
UNROLL = 4
HIDDEN_SCORE = -1e30
SCORE_SCALE = math.log2(math.e) / math.sqrt(HEAD_DIM)

CTX = ("x", "zl")
EXP = ("yh", "yl", "zh", "c")
ALL = CTX + EXP
PARTS = (4, 2, 2, 2, 2, 2)
OWNER = ("yl", "zh", "c", "yh")

CORE_SWAP = [(0, 1), (1, 0)]
Z_FLIP = [(0, 3), (3, 0), (1, 2), (2, 1)]
CAPACITY = 16
SLOT_TILE = 256
WIDTH_TILE = 512
VMEM_LIMIT = 60 << 20


def attend_kernel(block, scalars, q_ref, mine_ref, other_ref, o_ref, *scratch):
    kv, max_ref, total_ref, sum_ref, score_ref, sems = scratch
    step = pl.program_id(0)
    ctx = scalars[SEGS]
    core = scalars[SEGS + 1]
    half = block // 2

    def fetch(b):
        return [
            pltpu.make_async_copy(
                piece.at[b, pl.ds(2 * TILE, half), :],
                kv.at[pl.ds(pl.multiple_of(KEY_TILE + b * block + side * half, half), half), :],
                sems.at[i, b],
            )
            for i, (piece, side) in enumerate(((mine_ref, core), (other_ref, 1 - core)))
        ]

    @pl.when(step == 0)
    def _():
        for b in range(8):
            for copy in fetch(b):
                copy.start()
        kv[:KEY_TILE, :] = jnp.zeros((KEY_TILE, 2 * HEAD_DIM), kv.dtype)

    for b in range(8):

        @pl.when(step == 2 * b)
        def _(b=b):
            for copy in fetch(b):
                copy.wait()

    begin = (step // 2) * block + (step % 2) * half + ctx * TILE
    end = begin + TILE
    lowest_first = jnp.int32(0)
    for s in range(SEGS):
        lowest_first = jnp.where(scalars[s] <= begin, scalars[s], lowest_first)
    chunks = (end - lowest_first + KEY_TILE - 1) // KEY_TILE

    query = jnp.concatenate([q_ref[:, :HEAD_DIM], q_ref[:, HEAD_DIM:]], axis=0)
    position = begin + lax.broadcasted_iota(jnp.int32, (TILE, HEAD_DIM), 0)
    lowest = jnp.zeros((TILE, HEAD_DIM), jnp.int32)
    for s in range(SEGS):
        lowest = jnp.where(position >= scalars[s], scalars[s], lowest)
    wide = KEY_TILE // HEAD_DIM
    lane = lax.broadcasted_iota(jnp.int32, (TILE, KEY_TILE), 1)
    lowest = jnp.concatenate([lowest] * wide, axis=1) - lane
    position = jnp.concatenate([position] * wide, axis=1) - lane

    max_ref[...] = jnp.full_like(max_ref, HIDDEN_SCORE)
    total_ref[...] = jnp.zeros_like(total_ref)
    sum_ref[...] = jnp.zeros_like(sum_ref)

    def rows_of(chunk):
        return pl.ds(pl.multiple_of(end - chunk * KEY_TILE, TILE), KEY_TILE)

    def score(slot, chunk):
        score_ref[slot] = lax.dot_general(
            query,
            kv[rows_of(chunk), :HEAD_DIM],
            (((1,), (1,)), ((), ())),
            preferred_element_type=jnp.float32,
        )

    def accumulate(slot, chunk):
        first = end - (chunk + 1) * KEY_TILE
        visible = (lowest <= first) & (position >= first)
        scores = jnp.where(
            jnp.concatenate([visible, visible], axis=0), score_ref[slot] * SCORE_SCALE, HIDDEN_SCORE
        )
        old_max = max_ref[...]
        new_max = jnp.maximum(old_max, jnp.max(scores, axis=1, keepdims=True))
        rescale = jnp.exp2(old_max - new_max)
        unnormed = jnp.exp2(scores - jnp.concatenate([new_max] * wide, axis=1))
        total_ref[...] = rescale * total_ref[...] + jnp.sum(unnormed, axis=1, keepdims=True)
        max_ref[...] = new_max
        sum_ref[...] = rescale * sum_ref[...] + jnp.dot(
            unnormed.astype(jnp.bfloat16),
            kv[rows_of(chunk), HEAD_DIM:],
            preferred_element_type=jnp.float32,
        )

    last = chunks - 1
    score(0, 0)

    def run(first, count):
        for i in range(count):
            score((i + 1) % 2, jnp.minimum(first + i + 1, last))
            accumulate(i % 2, first + i)

    @pl.loop(0, chunks // UNROLL)
    def _(i):
        run(UNROLL * i, UNROLL)

    if UNROLL == 4:

        @pl.when(chunks % 4 >= 2)
        def _():
            run(chunks // 4 * 4, 2)

    @pl.when(chunks % 2 == 1)
    def _():
        accumulate(0, last)

    attended = (sum_ref[...] / total_ref[...]).astype(o_ref.dtype)
    o_ref[:, :HEAD_DIM] = attended[:TILE]
    o_ref[:, HEAD_DIM:] = attended[TILE:]


def gather_keys(queries, key_rows, value_rows, y, c):
    block, columns = queries.shape
    half = block // 2
    own = jnp.concatenate(
        [
            lax.dynamic_slice(rows, (c * half, y * HEAD_DIM), (half, HEAD_DIM))
            for rows in (key_rows, value_rows)
        ],
        axis=1,
    )
    striped = jnp.transpose(queries.reshape(2, 8, TILE, columns), (1, 0, 2, 3))
    sent = jnp.concatenate(
        [
            striped.reshape(8, 2 * TILE, columns),
            jnp.broadcast_to(own, (8, half, columns)),
        ],
        axis=1,
    )
    mine = lax.all_to_all(sent, CTX, split_axis=0, concat_axis=0, tiled=True)
    other = lax.ppermute(mine, "c", CORE_SWAP)
    return mine, other


def attend(scalars, mine, other, block):
    columns = mine.shape[2]
    any_spec = pl.BlockSpec(memory_space=pl.ANY)
    tile_spec = pl.BlockSpec((None, TILE, columns), lambda i, s: (i // 2, i % 2, 0))
    return pl.pallas_call(
        lambda *refs: attend_kernel(block, *refs),
        out_shape=jax.ShapeDtypeStruct((8, 2 * TILE, columns), jnp.bfloat16),
        grid_spec=pltpu.PrefetchScalarGridSpec(
            num_scalar_prefetch=1,
            grid=(16,),
            in_specs=[tile_spec, any_spec, any_spec],
            out_specs=tile_spec,
            scratch_shapes=[
                pltpu.VMEM((KEY_TILE + 8 * block, 2 * HEAD_DIM), jnp.bfloat16),
                pltpu.VMEM((2 * TILE, HEAD_DIM), jnp.float32),
                pltpu.VMEM((2 * TILE, HEAD_DIM), jnp.float32),
                pltpu.VMEM((2 * TILE, HEAD_DIM), jnp.float32),
                pltpu.VMEM((2, 2 * TILE, KEY_TILE), jnp.float32),
                pltpu.SemaphoreType.DMA((2, 8)),
            ],
        ),
        compiler_params=pltpu.CompilerParams(vmem_limit_bytes=VMEM_LIMIT),
        cost_estimate=pl.CostEstimate(
            flops=8 << 30, bytes_accessed=12 << 20, transcendentals=16 << 20
        ),
        name="attend",
    )(scalars, mine, mine, other)


def place_rows(slots_ref, normed, first, out_ref):
    count, rows = out_ref.shape[0], normed.shape[0]
    slot = first + lax.broadcasted_iota(jnp.int32, (count, rows), 0)
    chosen = slots_ref[0:1, :] == slot
    for k in range(1, TOP):
        chosen = chosen | (slots_ref[k : k + 1, :] == slot)
    onehot = jnp.where(chosen, 1.0, 0.0).astype(jnp.bfloat16)
    out_ref[...] = jnp.dot(onehot, normed, preferred_element_type=jnp.float32).astype(
        out_ref.dtype
    )


def mix_kernel(scalars, attended_ref, w0, w1, w2, w3, residual_ref, gain_ref, slots_ref, *refs):
    mixed_ref, normed_ref, outgoing_ref = refs
    step = pl.program_id(0)
    tiles = mixed_ref.shape[1] // WIDTH_TILE

    for n in range(tiles):

        @pl.when(step == n)
        def _(n=n):
            columns = slice(n * WIDTH_TILE, (n + 1) * WIDTH_TILE)
            total = residual_ref[:, columns].astype(jnp.float32)
            for p, w_ref in enumerate((w0, w1, w2, w3)):
                rows = jnp.concatenate(
                    [attended_ref[k % 2 * 8 + scalars[p] * 2 + k // 2] for k in range(4)],
                    axis=1,
                )
                total += jnp.dot(rows, w_ref[...], preferred_element_type=jnp.float32)
            mixed_ref[:, columns] = total

    @pl.when(step == tiles - 1)
    def _():
        mixed = mixed_ref[...]
        mean_square = jnp.mean(mixed * mixed, axis=-1, keepdims=True)
        normed_ref[...] = (mixed * lax.rsqrt(mean_square + 1e-06) * gain_ref[...]).astype(
            jnp.bfloat16
        )

    @pl.when(step >= tiles)
    def _():
        place_rows(slots_ref, normed_ref[...], (step - tiles) * SLOT_TILE, outgoing_ref)


def whole(shape):
    return pl.BlockSpec(shape, lambda i, *s: (0,) * len(shape))


def mix(attended, weights, order, residual, norm_gain, slots):
    rows, width = residual.shape
    tiles = width // WIDTH_TILE
    count = 128 * CAPACITY // 2

    return pl.pallas_call(
        mix_kernel,
        out_shape=(
            jax.ShapeDtypeStruct((rows, width), jnp.float32),
            jax.ShapeDtypeStruct((rows, width), jnp.bfloat16),
            jax.ShapeDtypeStruct((count, width), jnp.bfloat16),
        ),
        grid_spec=pltpu.PrefetchScalarGridSpec(
            num_scalar_prefetch=1,
            grid=(tiles + count // SLOT_TILE,),
            in_specs=[whole(attended.shape)]
            + [
                pl.BlockSpec((1024, WIDTH_TILE), lambda i, s: (0, jnp.minimum(i, tiles - 1)))
                for _ in weights
            ]
            + [whole((rows, width)), whole((1, width)), whole((TOP, rows))],
            out_specs=(
                whole((rows, width)),
                whole((rows, width)),
                pl.BlockSpec((SLOT_TILE, width), lambda i, s: (jnp.maximum(i - tiles, 0), 0)),
            ),
        ),
        compiler_params=pltpu.CompilerParams(vmem_limit_bytes=VMEM_LIMIT),
        cost_estimate=pl.CostEstimate(
            flops=3 << 30, bytes_accessed=24 << 20, transcendentals=0
        ),
        name="mix",
    )(order, attended, *weights, residual, norm_gain.reshape(1, width), slots)


def place(normed, slots, first):
    rows, width = normed.shape
    count = 128 * CAPACITY // 2

    def kernel(normed_ref, slots_ref, out_ref):
        place_rows(
            slots_ref, normed_ref[...], first + pl.program_id(0) * SLOT_TILE, out_ref
        )

    return pl.pallas_call(
        kernel,
        out_shape=jax.ShapeDtypeStruct((count, width), jnp.bfloat16),
        grid=(count // SLOT_TILE,),
        in_specs=[whole((rows, width)), whole((TOP, rows))],
        out_specs=pl.BlockSpec((SLOT_TILE, width), lambda i: (i, 0)),
        compiler_params=pltpu.CompilerParams(vmem_limit_bytes=VMEM_LIMIT),
        cost_estimate=pl.CostEstimate(
            flops=1 << 29, bytes_accessed=5 << 20, transcendentals=0
        ),
        name="place",
    )(normed, slots)


def share_rows(slots_ref, route_ref, first, count):
    rows = slots_ref.shape[0]
    slot = first + lax.broadcasted_iota(jnp.int32, (rows, count), 1)
    share = jnp.zeros((rows, count), jnp.float32)
    for k in range(TOP):
        share = jnp.where(slots_ref[:, k : k + 1] == slot, route_ref[:, k : k + 1], share)
    high = share.astype(jnp.bfloat16)
    low = (share - high.astype(jnp.float32)).astype(jnp.bfloat16)
    return jnp.concatenate([high, low], axis=0)


def add_routed(shares, returned_ref, base_ref, out_ref):
    rows = base_ref.shape[0]
    both = jnp.dot(shares, returned_ref[...], preferred_element_type=jnp.float32)
    out_ref[...] = (base_ref[...] + (both[:rows] + both[rows:])).astype(out_ref.dtype)


def column_tile(height):
    return pl.BlockSpec((height, WIDTH_TILE), lambda i: (0, i))


COMBINE_PARAMS = dict(
    compiler_params=pltpu.CompilerParams(vmem_limit_bytes=VMEM_LIMIT),
    cost_estimate=pl.CostEstimate(flops=1 << 30, bytes_accessed=6 << 20, transcendentals=0),
)


def combine_first(returned, slots, route_weight, base):
    rows, width = base.shape
    count = returned.shape[0]

    def kernel(returned_ref, slots_ref, route_ref, base_ref, out_ref, late_ref, shares):
        @pl.when(pl.program_id(0) == 0)
        def _():
            shares[...] = share_rows(slots_ref, route_ref, 0, count)
            late_ref[...] = share_rows(slots_ref, route_ref, count, count)

        add_routed(shares[...], returned_ref, base_ref, out_ref)

    return pl.pallas_call(
        kernel,
        out_shape=(
            jax.ShapeDtypeStruct((rows, width), jnp.float32),
            jax.ShapeDtypeStruct((2 * rows, count), jnp.bfloat16),
        ),
        grid=(width // WIDTH_TILE,),
        in_specs=[column_tile(count), whole((rows, TOP)), whole((rows, TOP)), column_tile(rows)],
        out_specs=(column_tile(rows), whole((2 * rows, count))),
        scratch_shapes=[pltpu.VMEM((2 * rows, count), jnp.bfloat16)],
        name="combine_first",
        **COMBINE_PARAMS,
    )(returned, slots, route_weight, base)


def combine_last(returned, shares, base):
    rows, width = base.shape
    count = returned.shape[0]

    def kernel(returned_ref, shares_ref, base_ref, out_ref):
        add_routed(shares_ref[...], returned_ref, base_ref, out_ref)

    return pl.pallas_call(
        kernel,
        out_shape=jax.ShapeDtypeStruct((rows, width), jnp.bfloat16),
        grid=(width // WIDTH_TILE,),
        in_specs=[column_tile(count), whole((2 * rows, count)), column_tile(rows)],
        out_specs=column_tile(rows),
        name="combine_last",
        **COMBINE_PARAMS,
    )(returned, shares, base)


def expert_rows(arrived, gate_weight, up_weight, down_weight):
    in_shape = arrived.shape
    flat_rows = arrived.reshape(-1, in_shape[-1])
    gate_proj = jnp.dot(flat_rows, gate_weight[0], preferred_element_type=jnp.float32)
    up_proj = jnp.dot(flat_rows, up_weight[0], preferred_element_type=jnp.float32)
    hidden = (jax.nn.silu(gate_proj) * up_proj).astype(jnp.bfloat16)
    produced = jnp.dot(hidden, down_weight[0], preferred_element_type=jnp.float32).astype(
        jnp.bfloat16
    )
    return produced.reshape(in_shape)


def shards(
    residual,
    queries,
    key_rows,
    value_rows,
    segment_ids,
    out_weight,
    norm_gain,
    expert_ids,
    route_weight,
    gate_weight,
    up_weight,
    down_weight,
):
    columns = queries.shape[1]
    x, zl, yh, yl, zh, c = (lax.axis_index(name) for name in ALL)
    near = lax.all_gather(out_weight, ("yh", "yl"), axis=0, tiled=True)
    near_other = lax.ppermute(near, "c", CORE_SWAP)
    order = jnp.stack(
        [zh * 2 + c, zh * 2 + 1 - c, (1 - zh) * 2 + c, (1 - zh) * 2 + 1 - c]
    ).astype(jnp.int32)

    flat_ids = expert_ids.reshape(-1)
    onehot = (flat_ids[:, None] == jnp.arange(128, dtype=jnp.int32)[None, :]).astype(jnp.int32)
    slot_index = jnp.sum(jnp.cumsum(onehot, axis=0) * onehot, axis=1) - 1
    half = CAPACITY // 2
    slots = (
        slot_index // half * (128 * half) + flat_ids * half + slot_index % half
    ).reshape(expert_ids.shape)

    counts = jnp.sum(
        segment_ids[None, :] < jnp.arange(SEGS, dtype=jnp.int32)[:, None], axis=1, dtype=jnp.int32
    )
    starts = lax.psum(counts, CTX)
    mine, other = gather_keys(queries, key_rows, value_rows, yh * 2 + yl, c)
    late_weight, mine = lax.optimization_barrier((out_weight, mine))
    far = lax.ppermute(late_weight, ("zl", "zh"), Z_FLIP)
    far, starts, other = lax.optimization_barrier((far, starts, other))
    far = lax.all_gather(far, ("yh", "yl"), axis=0, tiled=True)
    scalars = jnp.concatenate([starts, jnp.stack([x * 2 + zl, c]).astype(jnp.int32)])
    attended = attend(scalars, mine, other, queries.shape[0])
    attended = lax.all_to_all(attended, CTX, split_axis=0, concat_axis=0, tiled=True)
    attended, far = lax.optimization_barrier((attended, far))
    far_other = lax.ppermute(far, "c", CORE_SWAP)
    attended = lax.all_to_all(
        attended.reshape(16, TILE, columns), OWNER, split_axis=0, concat_axis=0, tiled=True
    )
    mixed, normed, outgoing = mix(
        attended, (near, near_other, far, far_other), order, residual, norm_gain, slots.T
    )
    count, width = outgoing.shape

    def exchange(rows):
        return lax.all_to_all(
            rows.reshape(128, half, width), ALL, split_axis=0, concat_axis=0, tiled=True
        )

    def experts(rows):
        return expert_rows(rows, gate_weight, up_weight, down_weight)

    arrived_0 = exchange(outgoing)
    arrived_1 = exchange(place(normed, slots.T, count))
    returned_0 = exchange(experts(arrived_0)).reshape(count, width)
    returned_1 = exchange(experts(arrived_1)).reshape(count, width)
    partial, shares = combine_first(returned_0, slots, route_weight, mixed)
    return combine_last(returned_1, shares, partial)


def solution(mesh):
    fine = Mesh(mesh.devices.reshape(PARTS), ALL)
    return jax.shard_map(
        shards,
        mesh=fine,
        in_specs=(
            P(ALL, None),
            P(CTX, EXP),
            P(CTX, None),
            P(CTX, None),
            P(CTX),
            P(EXP, None),
            P(),
            P(ALL, None),
            P(ALL, None),
            P(ALL, None, None),
            P(ALL, None, None),
            P(ALL, None, None),
        ),
        out_specs=P(ALL, None),
        check_vma=False,
    )
```

```python
import math

import jax
import jax.numpy as jnp
from jax import lax
from jax.experimental import pallas as pl
from jax.experimental.pallas import tpu as pltpu
from jax.sharding import Mesh
from jax.sharding import PartitionSpec as P

HEAD_DIM = 128
TOP = 8
SEGS = 32
TILE = 128
KEY_TILE = 512
UNROLL = 4
HIDDEN_SCORE = -1e30
SCORE_SCALE = math.log2(math.e) / math.sqrt(HEAD_DIM)

CTX = ("x", "zl")
EXP = ("yh", "yl", "zh", "c")
ALL = CTX + EXP
PARTS = (4, 2, 2, 2, 2, 2)
OWNER = ("yl", "zh", "c", "yh")

CORE_SWAP = [(0, 1), (1, 0)]
Z_FLIP = [(0, 3), (3, 0), (1, 2), (2, 1)]
CAPACITY = 16
SLOT_TILE = 256
WIDTH_TILE = 512
VMEM_LIMIT = 60 << 20


def attend_kernel(block, scalars, q_ref, mine_ref, other_ref, o_ref, *scratch):
    kv, max_ref, total_ref, sum_ref, score_ref, sems = scratch
    step = pl.program_id(0)
    ctx = scalars[SEGS]
    core = scalars[SEGS + 1]
    half = block // 2

    def fetch(b):
        return [
            pltpu.make_async_copy(
                piece.at[b, pl.ds(2 * TILE, half), :],
                kv.at[pl.ds(pl.multiple_of(KEY_TILE + b * block + side * half, half), half), :],
                sems.at[i, b],
            )
            for i, (piece, side) in enumerate(((mine_ref, core), (other_ref, 1 - core)))
        ]

    @pl.when(step == 0)
    def _():
        for b in range(8):
            for copy in fetch(b):
                copy.start()
        kv[:KEY_TILE, :] = jnp.zeros((KEY_TILE, 2 * HEAD_DIM), kv.dtype)

    for b in range(8):

        @pl.when(step == 2 * b)
        def _(b=b):
            for copy in fetch(b):
                copy.wait()

    begin = (step // 2) * block + (step % 2) * half + ctx * TILE
    end = begin + TILE
    lowest_first = jnp.int32(0)
    for s in range(SEGS):
        lowest_first = jnp.where(scalars[s] <= begin, scalars[s], lowest_first)
    chunks = (end - lowest_first + KEY_TILE - 1) // KEY_TILE

    query = jnp.concatenate([q_ref[:, :HEAD_DIM], q_ref[:, HEAD_DIM:]], axis=0)
    position = begin + lax.broadcasted_iota(jnp.int32, (TILE, HEAD_DIM), 0)
    lowest = jnp.zeros((TILE, HEAD_DIM), jnp.int32)
    for s in range(SEGS):
        lowest = jnp.where(position >= scalars[s], scalars[s], lowest)
    wide = KEY_TILE // HEAD_DIM
    lane = lax.broadcasted_iota(jnp.int32, (TILE, KEY_TILE), 1)
    lowest = jnp.concatenate([lowest] * wide, axis=1) - lane
    position = jnp.concatenate([position] * wide, axis=1) - lane

    max_ref[...] = jnp.full_like(max_ref, HIDDEN_SCORE)
    total_ref[...] = jnp.zeros_like(total_ref)
    sum_ref[...] = jnp.zeros_like(sum_ref)

    def rows_of(chunk):
        return pl.ds(pl.multiple_of(end - chunk * KEY_TILE, TILE), KEY_TILE)

    def score(slot, chunk):
        score_ref[slot] = lax.dot_general(
            query,
            kv[rows_of(chunk), :HEAD_DIM],
            (((1,), (1,)), ((), ())),
            preferred_element_type=jnp.float32,
        )

    def accumulate(slot, chunk):
        first = end - (chunk + 1) * KEY_TILE
        visible = (lowest <= first) & (position >= first)
        scores = jnp.where(
            jnp.concatenate([visible, visible], axis=0), score_ref[slot] * SCORE_SCALE, HIDDEN_SCORE
        )
        old_max = max_ref[...]
        new_max = jnp.maximum(old_max, jnp.max(scores, axis=1, keepdims=True))
        rescale = jnp.exp2(old_max - new_max)
        unnormed = jnp.exp2(scores - jnp.concatenate([new_max] * wide, axis=1))
        total_ref[...] = rescale * total_ref[...] + jnp.sum(unnormed, axis=1, keepdims=True)
        max_ref[...] = new_max
        sum_ref[...] = rescale * sum_ref[...] + jnp.dot(
            unnormed.astype(jnp.bfloat16),
            kv[rows_of(chunk), HEAD_DIM:],
            preferred_element_type=jnp.float32,
        )

    last = chunks - 1
    score(0, 0)

    def run(first, count):
        for i in range(count):
            score((i + 1) % 2, jnp.minimum(first + i + 1, last))
            accumulate(i % 2, first + i)

    @pl.loop(0, chunks // UNROLL)
    def _(i):
        run(UNROLL * i, UNROLL)

    if UNROLL == 4:

        @pl.when(chunks % 4 >= 2)
        def _():
            run(chunks // 4 * 4, 2)

    @pl.when(chunks % 2 == 1)
    def _():
        accumulate(0, last)

    attended = (sum_ref[...] / total_ref[...]).astype(o_ref.dtype)
    o_ref[:, :HEAD_DIM] = attended[:TILE]
    o_ref[:, HEAD_DIM:] = attended[TILE:]


def gather_keys(queries, key_rows, value_rows, y, c):
    block, columns = queries.shape
    half = block // 2
    own = jnp.concatenate(
        [
            lax.dynamic_slice(rows, (c * half, y * HEAD_DIM), (half, HEAD_DIM))
            for rows in (key_rows, value_rows)
        ],
        axis=1,
    )
    striped = jnp.transpose(queries.reshape(2, 8, TILE, columns), (1, 0, 2, 3))
    sent = jnp.concatenate(
        [
            striped.reshape(8, 2 * TILE, columns),
            jnp.broadcast_to(own, (8, half, columns)),
        ],
        axis=1,
    )
    mine = lax.all_to_all(sent, CTX, split_axis=0, concat_axis=0, tiled=True)
    other = lax.ppermute(mine, "c", CORE_SWAP)
    return mine, other


def attend(scalars, mine, other, block):
    columns = mine.shape[2]
    any_spec = pl.BlockSpec(memory_space=pl.ANY)
    tile_spec = pl.BlockSpec((None, TILE, columns), lambda i, s: (i // 2, i % 2, 0))
    return pl.pallas_call(
        lambda *refs: attend_kernel(block, *refs),
        out_shape=jax.ShapeDtypeStruct((8, 2 * TILE, columns), jnp.bfloat16),
        grid_spec=pltpu.PrefetchScalarGridSpec(
            num_scalar_prefetch=1,
            grid=(16,),
            in_specs=[tile_spec, any_spec, any_spec],
            out_specs=tile_spec,
            scratch_shapes=[
                pltpu.VMEM((KEY_TILE + 8 * block, 2 * HEAD_DIM), jnp.bfloat16),
                pltpu.VMEM((2 * TILE, HEAD_DIM), jnp.float32),
                pltpu.VMEM((2 * TILE, HEAD_DIM), jnp.float32),
                pltpu.VMEM((2 * TILE, HEAD_DIM), jnp.float32),
                pltpu.VMEM((2, 2 * TILE, KEY_TILE), jnp.float32),
                pltpu.SemaphoreType.DMA((2, 8)),
            ],
        ),
        compiler_params=pltpu.CompilerParams(vmem_limit_bytes=VMEM_LIMIT),
        cost_estimate=pl.CostEstimate(
            flops=8 << 30, bytes_accessed=12 << 20, transcendentals=16 << 20
        ),
        name="attend",
    )(scalars, mine, mine, other)


def place_rows(slots_ref, normed, first, out_ref):
    count, rows = out_ref.shape[0], normed.shape[0]
    slot = first + lax.broadcasted_iota(jnp.int32, (count, rows), 0)
    chosen = slots_ref[0:1, :] == slot
    for k in range(1, TOP):
        chosen = chosen | (slots_ref[k : k + 1, :] == slot)
    onehot = jnp.where(chosen, 1.0, 0.0).astype(jnp.bfloat16)
    out_ref[...] = jnp.dot(onehot, normed, preferred_element_type=jnp.float32).astype(
        out_ref.dtype
    )


def mix_kernel(scalars, attended_ref, w0, w1, w2, w3, residual_ref, gain_ref, slots_ref, *refs):
    mixed_ref, normed_ref, outgoing_ref = refs
    step = pl.program_id(0)
    tiles = mixed_ref.shape[1] // WIDTH_TILE

    for n in range(tiles):

        @pl.when(step == n)
        def _(n=n):
            columns = slice(n * WIDTH_TILE, (n + 1) * WIDTH_TILE)
            total = residual_ref[:, columns].astype(jnp.float32)
            for p, w_ref in enumerate((w0, w1, w2, w3)):
                rows = jnp.concatenate(
                    [attended_ref[k % 2 * 8 + scalars[p] * 2 + k // 2] for k in range(4)],
                    axis=1,
                )
                total += jnp.dot(rows, w_ref[...], preferred_element_type=jnp.float32)
            mixed_ref[:, columns] = total

    @pl.when(step == tiles - 1)
    def _():
        mixed = mixed_ref[...]
        mean_square = jnp.mean(mixed * mixed, axis=-1, keepdims=True)
        normed_ref[...] = (mixed * lax.rsqrt(mean_square + 1e-06) * gain_ref[...]).astype(
            jnp.bfloat16
        )

    @pl.when(step >= tiles)
    def _():
        place_rows(slots_ref, normed_ref[...], (step - tiles) * SLOT_TILE, outgoing_ref)


def whole(shape):
    return pl.BlockSpec(shape, lambda i, *s: (0,) * len(shape))


def mix(attended, weights, order, residual, norm_gain, slots):
    rows, width = residual.shape
    tiles = width // WIDTH_TILE
    count = 128 * CAPACITY // 2

    return pl.pallas_call(
        mix_kernel,
        out_shape=(
            jax.ShapeDtypeStruct((rows, width), jnp.float32),
            jax.ShapeDtypeStruct((rows, width), jnp.bfloat16),
            jax.ShapeDtypeStruct((count, width), jnp.bfloat16),
        ),
        grid_spec=pltpu.PrefetchScalarGridSpec(
            num_scalar_prefetch=1,
            grid=(tiles + count // SLOT_TILE,),
            in_specs=[whole(attended.shape)]
            + [
                pl.BlockSpec((1024, WIDTH_TILE), lambda i, s: (0, jnp.minimum(i, tiles - 1)))
                for _ in weights
            ]
            + [whole((rows, width)), whole((1, width)), whole((TOP, rows))],
            out_specs=(
                whole((rows, width)),
                whole((rows, width)),
                pl.BlockSpec((SLOT_TILE, width), lambda i, s: (jnp.maximum(i - tiles, 0), 0)),
            ),
        ),
        compiler_params=pltpu.CompilerParams(vmem_limit_bytes=VMEM_LIMIT),
        cost_estimate=pl.CostEstimate(
            flops=3 << 30, bytes_accessed=24 << 20, transcendentals=0
        ),
        name="mix",
    )(order, attended, *weights, residual, norm_gain.reshape(1, width), slots)


def place(normed, slots, first):
    rows, width = normed.shape
    count = 128 * CAPACITY // 2

    def kernel(normed_ref, slots_ref, out_ref):
        place_rows(
            slots_ref, normed_ref[...], first + pl.program_id(0) * SLOT_TILE, out_ref
        )

    return pl.pallas_call(
        kernel,
        out_shape=jax.ShapeDtypeStruct((count, width), jnp.bfloat16),
        grid=(count // SLOT_TILE,),
        in_specs=[whole((rows, width)), whole((TOP, rows))],
        out_specs=pl.BlockSpec((SLOT_TILE, width), lambda i: (i, 0)),
        compiler_params=pltpu.CompilerParams(vmem_limit_bytes=VMEM_LIMIT),
        cost_estimate=pl.CostEstimate(
            flops=1 << 29, bytes_accessed=5 << 20, transcendentals=0
        ),
        name="place",
    )(normed, slots)


def share_rows(slots_ref, route_ref, first, count):
    rows = slots_ref.shape[0]
    slot = first + lax.broadcasted_iota(jnp.int32, (rows, count), 1)
    share = jnp.zeros((rows, count), jnp.float32)
    for k in range(TOP):
        share = jnp.where(slots_ref[:, k : k + 1] == slot, route_ref[:, k : k + 1], share)
    high = share.astype(jnp.bfloat16)
    low = (share - high.astype(jnp.float32)).astype(jnp.bfloat16)
    return jnp.concatenate([high, low], axis=0)


def add_routed(shares, returned_ref, base_ref, out_ref):
    rows = base_ref.shape[0]
    both = jnp.dot(shares, returned_ref[...], preferred_element_type=jnp.float32)
    out_ref[...] = (base_ref[...] + (both[:rows] + both[rows:])).astype(out_ref.dtype)


def column_tile(height):
    return pl.BlockSpec((height, WIDTH_TILE), lambda i: (0, i))


COMBINE_PARAMS = dict(
    compiler_params=pltpu.CompilerParams(vmem_limit_bytes=VMEM_LIMIT),
    cost_estimate=pl.CostEstimate(flops=1 << 30, bytes_accessed=6 << 20, transcendentals=0),
)


def combine_first(returned, slots, route_weight, base):
    rows, width = base.shape
    count = returned.shape[0]

    def kernel(returned_ref, slots_ref, route_ref, base_ref, out_ref, late_ref, shares):
        @pl.when(pl.program_id(0) == 0)
        def _():
            shares[...] = share_rows(slots_ref, route_ref, 0, count)
            late_ref[...] = share_rows(slots_ref, route_ref, count, count)

        add_routed(shares[...], returned_ref, base_ref, out_ref)

    return pl.pallas_call(
        kernel,
        out_shape=(
            jax.ShapeDtypeStruct((rows, width), jnp.float32),
            jax.ShapeDtypeStruct((2 * rows, count), jnp.bfloat16),
        ),
        grid=(width // WIDTH_TILE,),
        in_specs=[column_tile(count), whole((rows, TOP)), whole((rows, TOP)), column_tile(rows)],
        out_specs=(column_tile(rows), whole((2 * rows, count))),
        scratch_shapes=[pltpu.VMEM((2 * rows, count), jnp.bfloat16)],
        name="combine_first",
        **COMBINE_PARAMS,
    )(returned, slots, route_weight, base)


def combine_last(returned, shares, base):
    rows, width = base.shape
    count = returned.shape[0]

    def kernel(returned_ref, shares_ref, base_ref, out_ref):
        add_routed(shares_ref[...], returned_ref, base_ref, out_ref)

    return pl.pallas_call(
        kernel,
        out_shape=jax.ShapeDtypeStruct((rows, width), jnp.bfloat16),
        grid=(width // WIDTH_TILE,),
        in_specs=[column_tile(count), whole((2 * rows, count)), column_tile(rows)],
        out_specs=column_tile(rows),
        name="combine_last",
        **COMBINE_PARAMS,
    )(returned, shares, base)


def expert_rows(arrived, gate_weight, up_weight, down_weight):
    in_shape = arrived.shape
    flat_rows = arrived.reshape(-1, in_shape[-1])
    gate_proj = jnp.dot(flat_rows, gate_weight[0], preferred_element_type=jnp.float32)
    up_proj = jnp.dot(flat_rows, up_weight[0], preferred_element_type=jnp.float32)
    hidden = (jax.nn.silu(gate_proj) * up_proj).astype(jnp.bfloat16)
    produced = jnp.dot(hidden, down_weight[0], preferred_element_type=jnp.float32).astype(
        jnp.bfloat16
    )
    return produced.reshape(in_shape)


def shards(
    residual,
    queries,
    key_rows,
    value_rows,
    segment_ids,
    out_weight,
    norm_gain,
    expert_ids,
    route_weight,
    gate_weight,
    up_weight,
    down_weight,
):
    columns = queries.shape[1]
    x, zl, yh, yl, zh, c = (lax.axis_index(name) for name in ALL)
    near = lax.all_gather(out_weight, ("yh", "yl"), axis=0, tiled=True)
    order = jnp.stack(
        [zh * 2 + c, zh * 2 + 1 - c, (1 - zh) * 2 + c, (1 - zh) * 2 + 1 - c]
    ).astype(jnp.int32)

    flat_ids = expert_ids.reshape(-1)
    onehot = (flat_ids[:, None] == jnp.arange(128, dtype=jnp.int32)[None, :]).astype(jnp.int32)
    slot_index = jnp.sum(jnp.cumsum(onehot, axis=0) * onehot, axis=1) - 1
    half = CAPACITY // 2
    slots = (
        slot_index // half * (128 * half) + flat_ids * half + slot_index % half
    ).reshape(expert_ids.shape)

    counts = jnp.sum(
        segment_ids[None, :] < jnp.arange(SEGS, dtype=jnp.int32)[:, None], axis=1, dtype=jnp.int32
    )
    starts = lax.psum(counts, CTX)
    mine, other = gather_keys(queries, key_rows, value_rows, yh * 2 + yl, c)
    late_weight, mine = lax.optimization_barrier((out_weight, mine))
    far = lax.ppermute(late_weight, ("zl", "zh"), Z_FLIP)
    far, starts = lax.optimization_barrier((far, starts))
    near_other = lax.ppermute(near, "c", CORE_SWAP)
    far = lax.all_gather(far, ("yh", "yl"), axis=0, tiled=True)
    scalars = jnp.concatenate([starts, jnp.stack([x * 2 + zl, c]).astype(jnp.int32)])
    attended = attend(scalars, mine, other, queries.shape[0])
    attended = lax.all_to_all(attended, CTX, split_axis=0, concat_axis=0, tiled=True)
    attended, far = lax.optimization_barrier((attended, far))
    far_other = lax.ppermute(far, "c", CORE_SWAP)
    attended = lax.all_to_all(
        attended.reshape(16, TILE, columns), OWNER, split_axis=0, concat_axis=0, tiled=True
    )
    mixed, normed, outgoing = mix(
        attended, (near, near_other, far, far_other), order, residual, norm_gain, slots.T
    )
    count, width = outgoing.shape

    def exchange(rows):
        return lax.all_to_all(
            rows.reshape(128, half, width), ALL, split_axis=0, concat_axis=0, tiled=True
        )

    def experts(rows):
        return expert_rows(rows, gate_weight, up_weight, down_weight)

    arrived_0 = exchange(outgoing)
    arrived_1 = exchange(place(normed, slots.T, count))
    returned_0 = exchange(experts(arrived_0)).reshape(count, width)
    returned_1 = exchange(experts(arrived_1)).reshape(count, width)
    partial, shares = combine_first(returned_0, slots, route_weight, mixed)
    return combine_last(returned_1, shares, partial)


def solution(mesh):
    fine = Mesh(mesh.devices.reshape(PARTS), ALL)
    return jax.shard_map(
        shards,
        mesh=fine,
        in_specs=(
            P(ALL, None),
            P(CTX, EXP),
            P(CTX, None),
            P(CTX, None),
            P(CTX),
            P(EXP, None),
            P(),
            P(ALL, None),
            P(ALL, None),
            P(ALL, None, None),
            P(ALL, None, None),
            P(ALL, None, None),
        ),
        out_specs=P(ALL, None),
        check_vma=False,
    )
```

```python
import math

import jax
import jax.numpy as jnp
from jax import lax
from jax.experimental import pallas as pl
from jax.experimental.pallas import tpu as pltpu
from jax.sharding import Mesh
from jax.sharding import PartitionSpec as P

HEAD_DIM = 128
TOP = 8
SEGS = 32
TILE = 128
KEY_TILE = 512
UNROLL = 4
HIDDEN_SCORE = -1e30
SCORE_SCALE = math.log2(math.e) / math.sqrt(HEAD_DIM)

CTX = ("x", "zl")
EXP = ("yh", "yl", "zh", "c")
ALL = CTX + EXP
PARTS = (4, 2, 2, 2, 2, 2)
OWNER = ("yl", "zh", "c", "yh")

CORE_SWAP = [(0, 1), (1, 0)]
Z_FLIP = [(0, 3), (3, 0), (1, 2), (2, 1)]
CAPACITY = 16
SLOT_TILE = 512
WIDTH_TILE = 1024
VMEM_LIMIT = 60 << 20


def attend_kernel(block, scalars, q_ref, mine_ref, other_ref, o_ref, *scratch):
    kv, max_ref, total_ref, sum_ref, score_ref, sems = scratch
    step = pl.program_id(0)
    ctx = scalars[SEGS]
    core = scalars[SEGS + 1]
    half = block // 2

    def fetch(b):
        return [
            pltpu.make_async_copy(
                piece.at[b, pl.ds(2 * TILE, half), :],
                kv.at[pl.ds(pl.multiple_of(KEY_TILE + b * block + side * half, half), half), :],
                sems.at[i, b],
            )
            for i, (piece, side) in enumerate(((mine_ref, core), (other_ref, 1 - core)))
        ]

    @pl.when(step == 0)
    def _():
        for b in range(8):
            for copy in fetch(b):
                copy.start()
        kv[:KEY_TILE, :] = jnp.zeros((KEY_TILE, 2 * HEAD_DIM), kv.dtype)

    for b in range(8):

        @pl.when(step == 2 * b)
        def _(b=b):
            for copy in fetch(b):
                copy.wait()

    begin = (step // 2) * block + (step % 2) * half + ctx * TILE
    end = begin + TILE
    lowest_first = jnp.int32(0)
    for s in range(SEGS):
        lowest_first = jnp.where(scalars[s] <= begin, scalars[s], lowest_first)
    chunks = (end - lowest_first + KEY_TILE - 1) // KEY_TILE

    query = jnp.concatenate([q_ref[:, :HEAD_DIM], q_ref[:, HEAD_DIM:]], axis=0)
    position = begin + lax.broadcasted_iota(jnp.int32, (TILE, HEAD_DIM), 0)
    lowest = jnp.zeros((TILE, HEAD_DIM), jnp.int32)
    for s in range(SEGS):
        lowest = jnp.where(position >= scalars[s], scalars[s], lowest)
    wide = KEY_TILE // HEAD_DIM
    lane = lax.broadcasted_iota(jnp.int32, (TILE, KEY_TILE), 1)
    lowest = jnp.concatenate([lowest] * wide, axis=1) - lane
    position = jnp.concatenate([position] * wide, axis=1) - lane

    max_ref[...] = jnp.full_like(max_ref, HIDDEN_SCORE)
    total_ref[...] = jnp.zeros_like(total_ref)
    sum_ref[...] = jnp.zeros_like(sum_ref)

    def rows_of(chunk):
        return pl.ds(pl.multiple_of(end - chunk * KEY_TILE, TILE), KEY_TILE)

    def score(slot, chunk):
        score_ref[slot] = lax.dot_general(
            query,
            kv[rows_of(chunk), :HEAD_DIM],
            (((1,), (1,)), ((), ())),
            preferred_element_type=jnp.float32,
        )

    def accumulate(slot, chunk):
        first = end - (chunk + 1) * KEY_TILE
        visible = (lowest <= first) & (position >= first)
        scores = jnp.where(
            jnp.concatenate([visible, visible], axis=0), score_ref[slot] * SCORE_SCALE, HIDDEN_SCORE
        )
        old_max = max_ref[...]
        new_max = jnp.maximum(old_max, jnp.max(scores, axis=1, keepdims=True))
        rescale = jnp.exp2(old_max - new_max)
        unnormed = jnp.exp2(scores - jnp.concatenate([new_max] * wide, axis=1))
        total_ref[...] = rescale * total_ref[...] + jnp.sum(unnormed, axis=1, keepdims=True)
        max_ref[...] = new_max
        sum_ref[...] = rescale * sum_ref[...] + jnp.dot(
            unnormed.astype(jnp.bfloat16),
            kv[rows_of(chunk), HEAD_DIM:],
            preferred_element_type=jnp.float32,
        )

    last = chunks - 1
    score(0, 0)

    def run(first, count):
        for i in range(count):
            score((i + 1) % 2, jnp.minimum(first + i + 1, last))
            accumulate(i % 2, first + i)

    @pl.loop(0, chunks // UNROLL)
    def _(i):
        run(UNROLL * i, UNROLL)

    if UNROLL == 4:

        @pl.when(chunks % 4 >= 2)
        def _():
            run(chunks // 4 * 4, 2)

    @pl.when(chunks % 2 == 1)
    def _():
        accumulate(0, last)

    attended = (sum_ref[...] / total_ref[...]).astype(o_ref.dtype)
    o_ref[:, :HEAD_DIM] = attended[:TILE]
    o_ref[:, HEAD_DIM:] = attended[TILE:]


def gather_keys(queries, key_rows, value_rows, y, c):
    block, columns = queries.shape
    half = block // 2
    own = jnp.concatenate(
        [
            lax.dynamic_slice(rows, (c * half, y * HEAD_DIM), (half, HEAD_DIM))
            for rows in (key_rows, value_rows)
        ],
        axis=1,
    )
    striped = jnp.transpose(queries.reshape(2, 8, TILE, columns), (1, 0, 2, 3))
    sent = jnp.concatenate(
        [
            striped.reshape(8, 2 * TILE, columns),
            jnp.broadcast_to(own, (8, half, columns)),
        ],
        axis=1,
    )
    mine = lax.all_to_all(sent, CTX, split_axis=0, concat_axis=0, tiled=True)
    other = lax.ppermute(mine, "c", CORE_SWAP)
    return mine, other


def attend(scalars, mine, other, block):
    columns = mine.shape[2]
    any_spec = pl.BlockSpec(memory_space=pl.ANY)
    tile_spec = pl.BlockSpec((None, TILE, columns), lambda i, s: (i // 2, i % 2, 0))
    return pl.pallas_call(
        lambda *refs: attend_kernel(block, *refs),
        out_shape=jax.ShapeDtypeStruct((8, 2 * TILE, columns), jnp.bfloat16),
        grid_spec=pltpu.PrefetchScalarGridSpec(
            num_scalar_prefetch=1,
            grid=(16,),
            in_specs=[tile_spec, any_spec, any_spec],
            out_specs=tile_spec,
            scratch_shapes=[
                pltpu.VMEM((KEY_TILE + 8 * block, 2 * HEAD_DIM), jnp.bfloat16),
                pltpu.VMEM((2 * TILE, HEAD_DIM), jnp.float32),
                pltpu.VMEM((2 * TILE, HEAD_DIM), jnp.float32),
                pltpu.VMEM((2 * TILE, HEAD_DIM), jnp.float32),
                pltpu.VMEM((2, 2 * TILE, KEY_TILE), jnp.float32),
                pltpu.SemaphoreType.DMA((2, 8)),
            ],
        ),
        compiler_params=pltpu.CompilerParams(vmem_limit_bytes=VMEM_LIMIT),
        cost_estimate=pl.CostEstimate(
            flops=20 << 30, bytes_accessed=12 << 20, transcendentals=16 << 20
        ),
        name="attend",
    )(scalars, mine, mine, other)


def place_rows(slots_ref, normed, first, out_ref):
    count, rows = out_ref.shape[0], normed.shape[0]
    slot = first + lax.broadcasted_iota(jnp.int32, (count, rows), 0)
    chosen = slots_ref[0:1, :] == slot
    for k in range(1, TOP):
        chosen = chosen | (slots_ref[k : k + 1, :] == slot)
    onehot = jnp.where(chosen, 1.0, 0.0).astype(jnp.bfloat16)
    out_ref[...] = jnp.dot(onehot, normed, preferred_element_type=jnp.float32).astype(
        out_ref.dtype
    )


def mix_kernel(scalars, attended_ref, w0, w1, w2, w3, residual_ref, gain_ref, slots_ref, *refs):
    mixed_ref, normed_ref, outgoing_ref = refs
    step = pl.program_id(0)
    tiles = mixed_ref.shape[1] // WIDTH_TILE

    for n in range(tiles):

        @pl.when(step == n)
        def _(n=n):
            columns = slice(n * WIDTH_TILE, (n + 1) * WIDTH_TILE)
            total = residual_ref[:, columns].astype(jnp.float32)
            for p, w_ref in enumerate((w0, w1, w2, w3)):
                halves = [slice(None)] if p < 2 else [slice(0, 128), slice(128, 256)]
                rows = jnp.concatenate(
                    [
                        attended_ref[k % 2 * 8 + scalars[p] * 2 + k // 2, :, part]
                        for part in halves
                        for k in range(4)
                    ],
                    axis=1,
                )
                total += jnp.dot(rows, w_ref[...], preferred_element_type=jnp.float32)
            mixed_ref[:, columns] = total

    @pl.when(step == tiles - 1)
    def _():
        mixed = mixed_ref[...]
        mean_square = jnp.mean(mixed * mixed, axis=-1, keepdims=True)
        normed_ref[...] = (mixed * lax.rsqrt(mean_square + 1e-06) * gain_ref[...]).astype(
            jnp.bfloat16
        )

    @pl.when(step >= tiles)
    def _():
        place_rows(slots_ref, normed_ref[...], (step - tiles) * SLOT_TILE, outgoing_ref)


def whole(shape):
    return pl.BlockSpec(shape, lambda i, *s: (0,) * len(shape))


def mix(attended, weights, order, residual, norm_gain, slots):
    rows, width = residual.shape
    tiles = width // WIDTH_TILE
    count = 128 * CAPACITY // 2

    return pl.pallas_call(
        mix_kernel,
        out_shape=(
            jax.ShapeDtypeStruct((rows, width), jnp.float32),
            jax.ShapeDtypeStruct((rows, width), jnp.bfloat16),
            jax.ShapeDtypeStruct((count, width), jnp.bfloat16),
        ),
        grid_spec=pltpu.PrefetchScalarGridSpec(
            num_scalar_prefetch=1,
            grid=(tiles + count // SLOT_TILE,),
            in_specs=[whole(attended.shape)]
            + [
                pl.BlockSpec((1024, WIDTH_TILE), lambda i, s: (0, jnp.minimum(i, tiles - 1)))
                for _ in weights
            ]
            + [whole((rows, width)), whole((1, width)), whole((TOP, rows))],
            out_specs=(
                whole((rows, width)),
                whole((rows, width)),
                pl.BlockSpec((SLOT_TILE, width), lambda i, s: (jnp.maximum(i - tiles, 0), 0)),
            ),
        ),
        compiler_params=pltpu.CompilerParams(vmem_limit_bytes=VMEM_LIMIT),
        cost_estimate=pl.CostEstimate(
            flops=3 << 30, bytes_accessed=24 << 20, transcendentals=0
        ),
        name="mix",
    )(order, attended, *weights, residual, norm_gain.reshape(1, width), slots)


def place(normed, slots, first):
    rows, width = normed.shape
    count = 128 * CAPACITY // 2

    def kernel(normed_ref, slots_ref, out_ref):
        place_rows(
            slots_ref, normed_ref[...], first + pl.program_id(0) * SLOT_TILE, out_ref
        )

    return pl.pallas_call(
        kernel,
        out_shape=jax.ShapeDtypeStruct((count, width), jnp.bfloat16),
        grid=(count // SLOT_TILE,),
        in_specs=[whole((rows, width)), whole((TOP, rows))],
        out_specs=pl.BlockSpec((SLOT_TILE, width), lambda i: (i, 0)),
        compiler_params=pltpu.CompilerParams(vmem_limit_bytes=VMEM_LIMIT),
        cost_estimate=pl.CostEstimate(
            flops=1 << 29, bytes_accessed=5 << 20, transcendentals=0
        ),
        name="place",
    )(normed, slots)


def share_rows(slots_ref, route_ref, first, count):
    rows = slots_ref.shape[0]
    slot = first + lax.broadcasted_iota(jnp.int32, (rows, count), 1)
    share = jnp.zeros((rows, count), jnp.float32)
    for k in range(TOP):
        share = jnp.where(slots_ref[:, k : k + 1] == slot, route_ref[:, k : k + 1], share)
    high = share.astype(jnp.bfloat16)
    low = (share - high.astype(jnp.float32)).astype(jnp.bfloat16)
    return jnp.concatenate([high, low], axis=0)


def add_routed(shares, returned_ref, base_ref, out_ref):
    rows = base_ref.shape[0]
    both = jnp.dot(shares, returned_ref[...], preferred_element_type=jnp.float32)
    out_ref[...] = (base_ref[...] + (both[:rows] + both[rows:])).astype(out_ref.dtype)


def column_tile(height):
    return pl.BlockSpec((height, WIDTH_TILE), lambda i: (0, i))


COMBINE_PARAMS = dict(
    compiler_params=pltpu.CompilerParams(vmem_limit_bytes=VMEM_LIMIT),
    cost_estimate=pl.CostEstimate(flops=1 << 30, bytes_accessed=6 << 20, transcendentals=0),
)


def combine_first(returned, slots, route_weight, base):
    rows, width = base.shape
    count = returned.shape[0]

    def kernel(returned_ref, slots_ref, route_ref, base_ref, out_ref, late_ref, shares):
        @pl.when(pl.program_id(0) == 0)
        def _():
            shares[...] = share_rows(slots_ref, route_ref, 0, count)
            late_ref[...] = share_rows(slots_ref, route_ref, count, count)

        add_routed(shares[...], returned_ref, base_ref, out_ref)

    return pl.pallas_call(
        kernel,
        out_shape=(
            jax.ShapeDtypeStruct((rows, width), jnp.float32),
            jax.ShapeDtypeStruct((2 * rows, count), jnp.bfloat16),
        ),
        grid=(width // WIDTH_TILE,),
        in_specs=[column_tile(count), whole((rows, TOP)), whole((rows, TOP)), column_tile(rows)],
        out_specs=(column_tile(rows), whole((2 * rows, count))),
        scratch_shapes=[pltpu.VMEM((2 * rows, count), jnp.bfloat16)],
        name="combine_first",
        **COMBINE_PARAMS,
    )(returned, slots, route_weight, base)


def combine_last(returned, shares, base):
    rows, width = base.shape
    count = returned.shape[0]

    def kernel(returned_ref, shares_ref, base_ref, out_ref):
        add_routed(shares_ref[...], returned_ref, base_ref, out_ref)

    return pl.pallas_call(
        kernel,
        out_shape=jax.ShapeDtypeStruct((rows, width), jnp.bfloat16),
        grid=(width // WIDTH_TILE,),
        in_specs=[column_tile(count), whole((2 * rows, count)), column_tile(rows)],
        out_specs=column_tile(rows),
        name="combine_last",
        **COMBINE_PARAMS,
    )(returned, shares, base)


def expert_rows(arrived, gate_weight, up_weight, down_weight):
    in_shape = arrived.shape
    flat_rows = arrived.reshape(-1, in_shape[-1])
    gate_proj = jnp.dot(flat_rows, gate_weight[0], preferred_element_type=jnp.float32)
    up_proj = jnp.dot(flat_rows, up_weight[0], preferred_element_type=jnp.float32)
    hidden = (jax.nn.silu(gate_proj) * up_proj).astype(jnp.bfloat16)
    produced = jnp.dot(hidden, down_weight[0], preferred_element_type=jnp.float32).astype(
        jnp.bfloat16
    )
    return produced.reshape(in_shape)


def shards(
    residual,
    queries,
    key_rows,
    value_rows,
    segment_ids,
    out_weight,
    norm_gain,
    expert_ids,
    route_weight,
    gate_weight,
    up_weight,
    down_weight,
):
    columns = queries.shape[1]
    x, zl, yh, yl, zh, c = (lax.axis_index(name) for name in ALL)
    near = lax.all_gather(out_weight, ("yh", "yl"), axis=0, tiled=True)
    order = jnp.stack(
        [zh * 2 + c, zh * 2 + 1 - c, (1 - zh) * 2 + c, (1 - zh) * 2 + 1 - c]
    ).astype(jnp.int32)

    flat_ids = expert_ids.reshape(-1)
    onehot = (flat_ids[:, None] == jnp.arange(128, dtype=jnp.int32)[None, :]).astype(jnp.int32)
    slot_index = jnp.sum(jnp.cumsum(onehot, axis=0) * onehot, axis=1) - 1
    half = CAPACITY // 2
    slots = (
        slot_index // half * (128 * half) + flat_ids * half + slot_index % half
    ).reshape(expert_ids.shape)

    counts = jnp.sum(
        segment_ids[None, :] < jnp.arange(SEGS, dtype=jnp.int32)[:, None], axis=1, dtype=jnp.int32
    )
    starts = lax.psum(counts, CTX)
    mine, other = gather_keys(queries, key_rows, value_rows, yh * 2 + yl, c)
    rows = out_weight.shape[0] // 2
    sent = lax.dynamic_slice_in_dim(out_weight, (1 - zl) * rows, rows, 0)
    sent, mine = lax.optimization_barrier((sent, mine))
    far = lax.ppermute(sent, ("zl", "zh"), Z_FLIP)
    far, starts = lax.optimization_barrier((far, starts))
    near_other = lax.ppermute(near, "c", CORE_SWAP)
    far = lax.all_gather(far, ("zl", "yh", "yl"), axis=0, tiled=True)
    scalars = jnp.concatenate([starts, jnp.stack([x * 2 + zl, c]).astype(jnp.int32)])
    attended = attend(scalars, mine, other, queries.shape[0])
    attended = lax.all_to_all(attended, CTX, split_axis=0, concat_axis=0, tiled=True)
    attended, far = lax.optimization_barrier((attended, far))
    far_other = lax.ppermute(far, "c", CORE_SWAP)
    attended = lax.all_to_all(
        attended.reshape(16, TILE, columns), OWNER, split_axis=0, concat_axis=0, tiled=True
    )
    mixed, normed, outgoing = mix(
        attended, (near, near_other, far, far_other), order, residual, norm_gain, slots.T
    )
    count, width = outgoing.shape

    def exchange(rows):
        return lax.all_to_all(
            rows.reshape(128, half, width), ALL, split_axis=0, concat_axis=0, tiled=True
        )

    def experts(rows):
        return expert_rows(rows, gate_weight, up_weight, down_weight)

    arrived_0 = exchange(outgoing)
    arrived_1 = exchange(place(normed, slots.T, count))
    returned_0 = exchange(experts(arrived_0)).reshape(count, width)
    returned_1 = exchange(experts(arrived_1)).reshape(count, width)
    partial, shares = combine_first(returned_0, slots, route_weight, mixed)
    return combine_last(returned_1, shares, partial)


def solution(mesh):
    fine = Mesh(mesh.devices.reshape(PARTS), ALL)
    return jax.shard_map(
        shards,
        mesh=fine,
        in_specs=(
            P(ALL, None),
            P(CTX, EXP),
            P(CTX, None),
            P(CTX, None),
            P(CTX),
            P(EXP, None),
            P(),
            P(ALL, None),
            P(ALL, None),
            P(ALL, None, None),
            P(ALL, None, None),
            P(ALL, None, None),
        ),
        out_specs=P(ALL, None),
        check_vma=False,
    )
```

```python
import math

import jax
import jax.numpy as jnp
from jax import lax
from jax.experimental import pallas as pl
from jax.experimental.pallas import tpu as pltpu
from jax.sharding import Mesh
from jax.sharding import PartitionSpec as P

HEAD_DIM = 128
TOP = 8
SEGS = 32
TILE = 128
KEY_TILE = 512
UNROLL = 4
HIDDEN_SCORE = -1e30
SCORE_SCALE = math.log2(math.e) / math.sqrt(HEAD_DIM)

CTX = ("x", "zl")
EXP = ("yh", "yl", "zh", "c")
ALL = CTX + EXP
PARTS = (4, 2, 2, 2, 2, 2)
OWNER = ("yl", "zh", "c", "yh")

CORE_SWAP = [(0, 1), (1, 0)]
Z_FLIP = [(0, 3), (3, 0), (1, 2), (2, 1)]
CAPACITY = 16
SLOT_TILE = 512
WIDTH_TILE = 1024
VMEM_LIMIT = 60 << 20


def attend_kernel(block, scalars, q_ref, mine_ref, other_ref, o_ref, *scratch):
    kv, max_ref, total_ref, sum_ref, score_ref, sems = scratch
    step = pl.program_id(0)
    ctx = scalars[SEGS]
    core = scalars[SEGS + 1]
    half = block // 2

    def fetch(b):
        return [
            pltpu.make_async_copy(
                piece.at[b, pl.ds(2 * TILE, half), :],
                kv.at[pl.ds(pl.multiple_of(KEY_TILE + b * block + side * half, half), half), :],
                sems.at[i, b],
            )
            for i, (piece, side) in enumerate(((mine_ref, core), (other_ref, 1 - core)))
        ]

    @pl.when(step == 0)
    def _():
        for b in range(8):
            for copy in fetch(b):
                copy.start()
        kv[:KEY_TILE, :] = jnp.zeros((KEY_TILE, 2 * HEAD_DIM), kv.dtype)

    for b in range(8):

        @pl.when(step == 2 * b)
        def _(b=b):
            for copy in fetch(b):
                copy.wait()

    begin = (step // 2) * block + (step % 2) * half + ctx * TILE
    end = begin + TILE
    lowest_first = jnp.int32(0)
    for s in range(SEGS):
        lowest_first = jnp.where(scalars[s] <= begin, scalars[s], lowest_first)
    chunks = (end - lowest_first + KEY_TILE - 1) // KEY_TILE

    query = jnp.concatenate([q_ref[:, :HEAD_DIM], q_ref[:, HEAD_DIM:]], axis=0)
    position = begin + lax.broadcasted_iota(jnp.int32, (TILE, HEAD_DIM), 0)
    lowest = jnp.zeros((TILE, HEAD_DIM), jnp.int32)
    for s in range(SEGS):
        lowest = jnp.where(position >= scalars[s], scalars[s], lowest)
    wide = KEY_TILE // HEAD_DIM
    lane = lax.broadcasted_iota(jnp.int32, (TILE, KEY_TILE), 1)
    lowest = jnp.concatenate([lowest] * wide, axis=1) - lane
    position = jnp.concatenate([position] * wide, axis=1) - lane

    max_ref[...] = jnp.full_like(max_ref, HIDDEN_SCORE)
    total_ref[...] = jnp.zeros_like(total_ref)
    sum_ref[...] = jnp.zeros_like(sum_ref)

    def rows_of(chunk):
        return pl.ds(pl.multiple_of(end - chunk * KEY_TILE, TILE), KEY_TILE)

    def score(slot, chunk):
        score_ref[slot] = lax.dot_general(
            query,
            kv[rows_of(chunk), :HEAD_DIM],
            (((1,), (1,)), ((), ())),
            preferred_element_type=jnp.float32,
        )

    def accumulate(slot, chunk):
        first = end - (chunk + 1) * KEY_TILE
        visible = (lowest <= first) & (position >= first)
        scores = jnp.where(
            jnp.concatenate([visible, visible], axis=0), score_ref[slot] * SCORE_SCALE, HIDDEN_SCORE
        )
        old_max = max_ref[...]
        new_max = jnp.maximum(old_max, jnp.max(scores, axis=1, keepdims=True))
        rescale = jnp.exp2(old_max - new_max)
        unnormed = jnp.exp2(scores - jnp.concatenate([new_max] * wide, axis=1))
        total_ref[...] = rescale * total_ref[...] + jnp.sum(unnormed, axis=1, keepdims=True)
        max_ref[...] = new_max
        sum_ref[...] = rescale * sum_ref[...] + jnp.dot(
            unnormed.astype(jnp.bfloat16),
            kv[rows_of(chunk), HEAD_DIM:],
            preferred_element_type=jnp.float32,
        )

    last = chunks - 1
    score(0, 0)

    def run(first, count):
        for i in range(count):
            score((i + 1) % 2, jnp.minimum(first + i + 1, last))
            accumulate(i % 2, first + i)

    @pl.loop(0, chunks // UNROLL)
    def _(i):
        run(UNROLL * i, UNROLL)

    if UNROLL == 4:

        @pl.when(chunks % 4 >= 2)
        def _():
            run(chunks // 4 * 4, 2)

    @pl.when(chunks % 2 == 1)
    def _():
        accumulate(0, last)

    attended = (sum_ref[...] / total_ref[...]).astype(o_ref.dtype)
    o_ref[:, :HEAD_DIM] = attended[:TILE]
    o_ref[:, HEAD_DIM:] = attended[TILE:]


def gather_keys(queries, key_rows, value_rows, y, c):
    block, columns = queries.shape
    half = block // 2
    own = jnp.concatenate(
        [
            lax.dynamic_slice(rows, (c * half, y * HEAD_DIM), (half, HEAD_DIM))
            for rows in (key_rows, value_rows)
        ],
        axis=1,
    )
    striped = jnp.transpose(queries.reshape(2, 8, TILE, columns), (1, 0, 2, 3))
    sent = jnp.concatenate(
        [
            striped.reshape(8, 2 * TILE, columns),
            jnp.broadcast_to(own, (8, half, columns)),
        ],
        axis=1,
    )
    mine = lax.all_to_all(sent, CTX, split_axis=0, concat_axis=0, tiled=True)
    other = lax.ppermute(mine, "c", CORE_SWAP)
    return mine, other


def attend(scalars, mine, other, block):
    columns = mine.shape[2]
    any_spec = pl.BlockSpec(memory_space=pl.ANY)
    tile_spec = pl.BlockSpec((None, TILE, columns), lambda i, s: (i // 2, i % 2, 0))
    return pl.pallas_call(
        lambda *refs: attend_kernel(block, *refs),
        out_shape=jax.ShapeDtypeStruct((8, 2 * TILE, columns), jnp.bfloat16),
        grid_spec=pltpu.PrefetchScalarGridSpec(
            num_scalar_prefetch=1,
            grid=(16,),
            in_specs=[tile_spec, any_spec, any_spec],
            out_specs=tile_spec,
            scratch_shapes=[
                pltpu.VMEM((KEY_TILE + 8 * block, 2 * HEAD_DIM), jnp.bfloat16),
                pltpu.VMEM((2 * TILE, HEAD_DIM), jnp.float32),
                pltpu.VMEM((2 * TILE, HEAD_DIM), jnp.float32),
                pltpu.VMEM((2 * TILE, HEAD_DIM), jnp.float32),
                pltpu.VMEM((2, 2 * TILE, KEY_TILE), jnp.float32),
                pltpu.SemaphoreType.DMA((2, 8)),
            ],
        ),
        compiler_params=pltpu.CompilerParams(vmem_limit_bytes=VMEM_LIMIT),
        cost_estimate=pl.CostEstimate(
            flops=20 << 30, bytes_accessed=12 << 20, transcendentals=16 << 20
        ),
        name="attend",
    )(scalars, mine, mine, other)


def place_rows(slots_ref, normed, first, out_ref):
    count, rows = out_ref.shape[0], normed.shape[0]
    slot = first + lax.broadcasted_iota(jnp.int32, (count, rows), 0)
    chosen = slots_ref[0:1, :] == slot
    for k in range(1, TOP):
        chosen = chosen | (slots_ref[k : k + 1, :] == slot)
    onehot = jnp.where(chosen, 1.0, 0.0).astype(jnp.bfloat16)
    out_ref[...] = jnp.dot(onehot, normed, preferred_element_type=jnp.float32).astype(
        out_ref.dtype
    )


def mix_kernel(scalars, attended_ref, w0, w1, w2, w3, residual_ref, gain_ref, slots_ref, *refs):
    mixed_ref, normed_ref, outgoing_ref = refs
    step = pl.program_id(0)
    tiles = mixed_ref.shape[1] // WIDTH_TILE

    for n in range(tiles):

        @pl.when(step == n)
        def _(n=n):
            columns = slice(n * WIDTH_TILE, (n + 1) * WIDTH_TILE)
            total = residual_ref[:, columns].astype(jnp.float32)
            for p, w_ref in enumerate((w0, w1, w2, w3)):
                halves = [slice(None)] if p < 2 else [slice(0, 128), slice(128, 256)]
                rows = jnp.concatenate(
                    [
                        attended_ref[k % 2 * 8 + scalars[p] * 2 + k // 2, :, part]
                        for part in halves
                        for k in range(4)
                    ],
                    axis=1,
                )
                total += jnp.dot(rows, w_ref[...], preferred_element_type=jnp.float32)
            mixed_ref[:, columns] = total

    @pl.when(step == tiles - 1)
    def _():
        mixed = mixed_ref[...]
        mean_square = jnp.mean(mixed * mixed, axis=-1, keepdims=True)
        normed_ref[...] = (mixed * lax.rsqrt(mean_square + 1e-06) * gain_ref[...]).astype(
            jnp.bfloat16
        )

    @pl.when(step >= tiles)
    def _():
        place_rows(slots_ref, normed_ref[...], (step - tiles) * SLOT_TILE, outgoing_ref)


def whole(shape):
    return pl.BlockSpec(shape, lambda i, *s: (0,) * len(shape))


def mix(attended, weights, order, residual, norm_gain, slots):
    rows, width = residual.shape
    tiles = width // WIDTH_TILE
    count = 128 * CAPACITY // 2

    return pl.pallas_call(
        mix_kernel,
        out_shape=(
            jax.ShapeDtypeStruct((rows, width), jnp.float32),
            jax.ShapeDtypeStruct((rows, width), jnp.bfloat16),
            jax.ShapeDtypeStruct((count, width), jnp.bfloat16),
        ),
        grid_spec=pltpu.PrefetchScalarGridSpec(
            num_scalar_prefetch=1,
            grid=(tiles + count // SLOT_TILE,),
            in_specs=[whole(attended.shape)]
            + [
                pl.BlockSpec((1024, WIDTH_TILE), lambda i, s: (0, jnp.minimum(i, tiles - 1)))
                for _ in weights
            ]
            + [whole((rows, width)), whole((1, width)), whole((TOP, rows))],
            out_specs=(
                whole((rows, width)),
                whole((rows, width)),
                pl.BlockSpec((SLOT_TILE, width), lambda i, s: (jnp.maximum(i - tiles, 0), 0)),
            ),
        ),
        compiler_params=pltpu.CompilerParams(vmem_limit_bytes=VMEM_LIMIT),
        cost_estimate=pl.CostEstimate(
            flops=3 << 30, bytes_accessed=24 << 20, transcendentals=0
        ),
        name="mix",
    )(order, attended, *weights, residual, norm_gain.reshape(1, width), slots)


def place(normed, slots, first):
    rows, width = normed.shape
    count = 128 * CAPACITY // 2

    def kernel(normed_ref, slots_ref, out_ref):
        place_rows(
            slots_ref, normed_ref[...], first + pl.program_id(0) * SLOT_TILE, out_ref
        )

    return pl.pallas_call(
        kernel,
        out_shape=jax.ShapeDtypeStruct((count, width), jnp.bfloat16),
        grid=(count // SLOT_TILE,),
        in_specs=[whole((rows, width)), whole((TOP, rows))],
        out_specs=pl.BlockSpec((SLOT_TILE, width), lambda i: (i, 0)),
        compiler_params=pltpu.CompilerParams(vmem_limit_bytes=VMEM_LIMIT),
        cost_estimate=pl.CostEstimate(
            flops=1 << 29, bytes_accessed=5 << 20, transcendentals=0
        ),
        name="place",
    )(normed, slots)


def share_rows(slots_ref, route_ref, first, count):
    rows = slots_ref.shape[0]
    slot = first + lax.broadcasted_iota(jnp.int32, (rows, count), 1)
    share = jnp.zeros((rows, count), jnp.float32)
    for k in range(TOP):
        share = jnp.where(slots_ref[:, k : k + 1] == slot, route_ref[:, k : k + 1], share)
    high = share.astype(jnp.bfloat16)
    low = (share - high.astype(jnp.float32)).astype(jnp.bfloat16)
    return jnp.concatenate([high, low], axis=0)


def add_routed(shares, returned_ref, base_ref, out_ref):
    rows = base_ref.shape[0]
    both = jnp.dot(shares, returned_ref[...], preferred_element_type=jnp.float32)
    out_ref[...] = (base_ref[...] + (both[:rows] + both[rows:])).astype(out_ref.dtype)


def column_tile(height):
    return pl.BlockSpec((height, WIDTH_TILE), lambda i: (0, i))


COMBINE_PARAMS = dict(
    compiler_params=pltpu.CompilerParams(vmem_limit_bytes=VMEM_LIMIT),
    cost_estimate=pl.CostEstimate(flops=1 << 30, bytes_accessed=6 << 20, transcendentals=0),
)


def combine_first(returned, slots, route_weight, base):
    rows, width = base.shape
    count = returned.shape[0]

    def kernel(returned_ref, slots_ref, route_ref, base_ref, out_ref, late_ref, shares):
        @pl.when(pl.program_id(0) == 0)
        def _():
            shares[...] = share_rows(slots_ref, route_ref, 0, count)
            late_ref[...] = share_rows(slots_ref, route_ref, count, count)

        add_routed(shares[...], returned_ref, base_ref, out_ref)

    return pl.pallas_call(
        kernel,
        out_shape=(
            jax.ShapeDtypeStruct((rows, width), jnp.float32),
            jax.ShapeDtypeStruct((2 * rows, count), jnp.bfloat16),
        ),
        grid=(width // WIDTH_TILE,),
        in_specs=[column_tile(count), whole((rows, TOP)), whole((rows, TOP)), column_tile(rows)],
        out_specs=(column_tile(rows), whole((2 * rows, count))),
        scratch_shapes=[pltpu.VMEM((2 * rows, count), jnp.bfloat16)],
        name="combine_first",
        **COMBINE_PARAMS,
    )(returned, slots, route_weight, base)


def combine_last(returned, shares, base):
    rows, width = base.shape
    count = returned.shape[0]

    def kernel(returned_ref, shares_ref, base_ref, out_ref):
        add_routed(shares_ref[...], returned_ref, base_ref, out_ref)

    return pl.pallas_call(
        kernel,
        out_shape=jax.ShapeDtypeStruct((rows, width), jnp.bfloat16),
        grid=(width // WIDTH_TILE,),
        in_specs=[column_tile(count), whole((2 * rows, count)), column_tile(rows)],
        out_specs=column_tile(rows),
        name="combine_last",
        **COMBINE_PARAMS,
    )(returned, shares, base)


def expert_rows(arrived, gate_weight, up_weight, down_weight):
    in_shape = arrived.shape
    flat_rows = arrived.reshape(-1, in_shape[-1])
    gate_proj = jnp.dot(flat_rows, gate_weight[0], preferred_element_type=jnp.float32)
    up_proj = jnp.dot(flat_rows, up_weight[0], preferred_element_type=jnp.float32)
    hidden = (jax.nn.silu(gate_proj) * up_proj).astype(jnp.bfloat16)
    produced = jnp.dot(hidden, down_weight[0], preferred_element_type=jnp.float32).astype(
        jnp.bfloat16
    )
    return produced.reshape(in_shape)


def shards(
    residual,
    queries,
    key_rows,
    value_rows,
    segment_ids,
    out_weight,
    norm_gain,
    expert_ids,
    route_weight,
    gate_weight,
    up_weight,
    down_weight,
):
    columns = queries.shape[1]
    x, zl, yh, yl, zh, c = (lax.axis_index(name) for name in ALL)
    near = lax.all_gather(out_weight, ("yh", "yl"), axis=0, tiled=True)
    order = jnp.stack(
        [zh * 2 + c, zh * 2 + 1 - c, (1 - zh) * 2 + c, (1 - zh) * 2 + 1 - c]
    ).astype(jnp.int32)

    flat_ids = expert_ids.reshape(-1)
    onehot = (flat_ids[:, None] == jnp.arange(128, dtype=jnp.int32)[None, :]).astype(jnp.int32)
    slot_index = jnp.sum(jnp.cumsum(onehot, axis=0) * onehot, axis=1) - 1
    half = CAPACITY // 2
    slots = (
        slot_index // half * (128 * half) + flat_ids * half + slot_index % half
    ).reshape(expert_ids.shape)

    counts = jnp.sum(
        segment_ids[None, :] < jnp.arange(SEGS, dtype=jnp.int32)[:, None], axis=1, dtype=jnp.int32
    )
    starts = lax.psum(counts, CTX)
    rows = out_weight.shape[0] // 2
    sent = lax.dynamic_slice_in_dim(out_weight, (1 - zl) * rows, rows, 0)
    queries, sent = lax.optimization_barrier((queries, sent))
    mine, other = gather_keys(queries, key_rows, value_rows, yh * 2 + yl, c)
    sent, mine = lax.optimization_barrier((sent, mine))
    far = lax.ppermute(sent, ("zl", "zh"), Z_FLIP)
    far, starts = lax.optimization_barrier((far, starts))
    near_other = lax.ppermute(near, "c", CORE_SWAP)
    far = lax.all_gather(far, ("zl", "yh", "yl"), axis=0, tiled=True)
    scalars = jnp.concatenate([starts, jnp.stack([x * 2 + zl, c]).astype(jnp.int32)])
    attended = attend(scalars, mine, other, queries.shape[0])
    attended = lax.all_to_all(attended, CTX, split_axis=0, concat_axis=0, tiled=True)
    attended, far = lax.optimization_barrier((attended, far))
    far_other = lax.ppermute(far, "c", CORE_SWAP)
    attended = lax.all_to_all(
        attended.reshape(16, TILE, columns), OWNER, split_axis=0, concat_axis=0, tiled=True
    )
    mixed, normed, outgoing = mix(
        attended, (near, near_other, far, far_other), order, residual, norm_gain, slots.T
    )
    count, width = outgoing.shape

    def exchange(rows):
        return lax.all_to_all(
            rows.reshape(128, half, width), ALL, split_axis=0, concat_axis=0, tiled=True
        )

    def experts(rows):
        return expert_rows(rows, gate_weight, up_weight, down_weight)

    arrived_0 = exchange(outgoing)
    arrived_1 = exchange(place(normed, slots.T, count))
    returned_0 = exchange(experts(arrived_0)).reshape(count, width)
    returned_1 = exchange(experts(arrived_1)).reshape(count, width)
    partial, shares = combine_first(returned_0, slots, route_weight, mixed)
    return combine_last(returned_1, shares, partial)


def solution(mesh):
    fine = Mesh(mesh.devices.reshape(PARTS), ALL)
    return jax.shard_map(
        shards,
        mesh=fine,
        in_specs=(
            P(ALL, None),
            P(CTX, EXP),
            P(CTX, None),
            P(CTX, None),
            P(CTX),
            P(EXP, None),
            P(),
            P(ALL, None),
            P(ALL, None),
            P(ALL, None, None),
            P(ALL, None, None),
            P(ALL, None, None),
        ),
        out_specs=P(ALL, None),
        check_vma=False,
    )
```
